32 devices in a mesh: parts: 2 (over x), row: 16 (over z, y, core).
Axes of the slice: x: 2, y: 2, z: 4, core: 2. Of those that a mesh axis runs over, the one named last changes fastest.
Arguments:
- raw_trace: float32 [320, 768, 512], P('row', 'parts'), parts along dimension 1, may hold values from -1200 to 1200
- fir_taps: float32 [32], replicated, may hold values from -1 to 1
- templ_real: bfloat16 [32, 320, 2048], P(None, None, 'row'), may hold values from -6 to 6
- templ_imag: bfloat16 [32, 320, 2048], P(None, None, 'row'), may hold values from -6 to 6
- channel_mask: int32 [320, 2048], P(None, 'row'), may hold values 0 or 1
- moveout: int32 [320, 2048], P(None, 'row'), may hold values from 0 to 63
Outputs:
- peak: float32 [2048, 768], P('row', 'parts'), parts along dimension 1
- best: float32 [768], P('parts'), parts along dimension 0
The draws below stay inside these ranges and needn't reach their ends.
There are 2 independent parts, one for each index of `parts`. The reference program is written for one: setup_inputs(seed, part) draws one part's arguments, and reference() takes and returns one part's arrays. A program takes and returns all parts, laid end to end along the dimension named above; an argument that names none is the same for every part. Nothing has to cross between parts.
All inputs are finite; a program needn't handle non-finite values. No bound on the sum of `channel_mask` on one device may be relied on, other than what follows from the above.
Results may differ from the reference program's by a relative error of at most 0.0015.
Values may be sent and summed in bfloat16 or wider, within the bound.
A program may use at most 128 MiB of HBM per device.

```python
import math
import jax
import jax.numpy as jnp
from jax import lax

CHANNELS = 320
SAMPLES = 256
BAND_BINS = 32
FIRST_BIN = 16
FILTER_TAPS = 32
MAX_MOVEOUT = 64
WINDOWS = 384
TEMPLATES = 2048


def draw_raw_trace(key, part):
    keys = jax.random.split(key, 3)
    ramp = 3.0 ** (jnp.arange(CHANNELS, dtype=jnp.float32) / max(CHANNELS - 1, 1))
    channel_gain = ramp * jnp.exp(jax.random.uniform(keys[0], (CHANNELS,), jnp.float32, 0.0, math.log(10.0)))
    window_gain = jnp.exp(jax.random.uniform(keys[1], (WINDOWS,), jnp.float32, 0.0, math.log(10.0)))
    shape = (CHANNELS, WINDOWS, 2 * SAMPLES)
    noise = jnp.clip(jax.random.normal(keys[2], shape, jnp.float32), -4.0, 4.0)
    return channel_gain[:, None, None] * window_gain[None, :, None] * noise


def set_ends(entries, rng, low, largest):
    place = [jax.random.randint(jax.random.fold_in(rng, axis), (), 0, length) for axis, length in enumerate(entries.shape)]
    widest = entries.shape.index(max(entries.shape))
    beside = place[:widest] + [(place[widest] + 1) % entries.shape[widest]] + place[widest + 1:]
    return entries.at[tuple(place)].set(low).at[tuple(beside)].set(largest)


def steps_of(key, extent, cuts, smallest, top_value):
    loudness, own = 1.0, jax.random.fold_in(key, 6)
    for axis_at, blocks in cuts:
        heights = jnp.exp(jax.random.uniform(jax.random.fold_in(own, axis_at), (blocks,), jnp.float32, smallest / len(cuts), top_value / len(cuts)))
        loudness = loudness * jnp.repeat(heights, extent[axis_at] // blocks).reshape([-1 if axis == axis_at else 1 for axis in range(len(extent))])
    return loudness


def normal_values(rng, extent, deviation, limit, cuts=(), kind=jnp.bfloat16):
    factor_of = steps_of(rng, extent, cuts, -0.22, 0.18) if cuts else 1.0
    result = jax.random.normal(rng, extent, jnp.float32) * deviation * factor_of
    return jnp.minimum(jnp.maximum(result, -limit), limit).astype(kind)


def setup_inputs(seed: int = 0, part: int = 0) -> dict:
    streams_of = jax.random.split(jax.random.key(seed), 7)
    part_splits = jax.random.split(jax.random.fold_in(streams_of[6], part), 7)
    return {
        "raw_trace": draw_raw_trace(jax.random.fold_in(jax.random.fold_in(streams_of[6], part), 71), part),
        "fir_taps": normal_values(streams_of[1], (FILTER_TAPS,), FILTER_TAPS ** -0.5, 1.0, (), jnp.float32),
        "templ_real": normal_values(streams_of[2], (BAND_BINS, CHANNELS, TEMPLATES), 1.0, 6.0, ((2, 16),)),
        "templ_imag": normal_values(streams_of[3], (BAND_BINS, CHANNELS, TEMPLATES), 1.0, 6.0, ((2, 16),)),
        "channel_mask": set_ends((jax.random.randint(streams_of[4], (CHANNELS, TEMPLATES), 0, 4) < 3).astype(jnp.int32), jax.random.fold_in(streams_of[4], 1), 0, 1),
        "moveout": set_ends(jax.random.randint(streams_of[5], (CHANNELS, TEMPLATES), 0, MAX_MOVEOUT), jax.random.fold_in(streams_of[5], 1), 0, MAX_MOVEOUT - 1).astype(jnp.int32),
    }


epsilon = 1e-06

def reference(raw_trace, fir_taps, templ_real, templ_imag, channel_mask, moveout):
    padded = jnp.pad(raw_trace, ((0, 0), (0, 0), (FILTER_TAPS - 1, 0)))
    decimated = jnp.zeros((CHANNELS, WINDOWS, SAMPLES), jnp.float32)
    for tap in range(FILTER_TAPS):
        begin = FILTER_TAPS - 1 - tap
        decimated = decimated + fir_taps[tap] * padded[:, :, begin:begin + 2 * SAMPLES:2]
    spectrum = jnp.fft.rfft(decimated, axis=-1)[:, :, FIRST_BIN:FIRST_BIN + BAND_BINS]
    spec_real = jnp.transpose(jnp.real(spectrum), (2, 0, 1)).astype(jnp.bfloat16)
    spec_imag = jnp.transpose(jnp.imag(spectrum), (2, 0, 1)).astype(jnp.bfloat16)
    real_wide = spec_real.astype(jnp.float32)
    imag_wide = spec_imag.astype(jnp.float32)
    energy = lax.optimization_barrier(jnp.sum(real_wide * real_wide + imag_wide * imag_wide, axis=(0, 1)))
    data_norm = jnp.sqrt(energy + epsilon)
    bin_index = FIRST_BIN + jnp.arange(BAND_BINS, dtype=jnp.int32)
    lag_index = jnp.arange(SAMPLES, dtype=jnp.int32)
    inverse_angle = 2.0 * math.pi / SAMPLES * (bin_index[:, None] * lag_index[None, :] % SAMPLES).astype(jnp.float32)
    inverse = jnp.concatenate([jnp.cos(inverse_angle), -jnp.sin(inverse_angle)], axis=0)
    scale = math.sqrt(2.0 * CHANNELS * BAND_BINS)
    block = math.gcd(TEMPLATES, 128)
    count = TEMPLATES // block

    def one_block(operands):
        real_block, imag_block, mask_block, shift_block = operands
        shift = bin_index[:, None, None] * shift_block[None, :, :] % SAMPLES
        phase = 2.0 * math.pi / SAMPLES * shift.astype(jnp.float32)
        cosine = jnp.cos(phase)
        sine = jnp.sin(phase)
        weight = mask_block.astype(jnp.float32)[None, :, :]
        real_in = real_block.astype(jnp.float32)
        imag_in = imag_block.astype(jnp.float32)
        eff_real = (weight * (real_in * cosine + imag_in * sine)).astype(jnp.bfloat16).astype(jnp.float32)
        eff_imag = (weight * (imag_in * cosine - real_in * sine)).astype(jnp.bfloat16).astype(jnp.float32)
        templ_norm = jnp.sqrt(lax.optimization_barrier(jnp.sum(eff_real * eff_real + eff_imag * eff_imag, axis=(0, 1))) + epsilon)
        cross_real = jnp.einsum('fct,fcw->ftw', eff_real, real_wide) + jnp.einsum('fct,fcw->ftw', eff_imag, imag_wide)
        cross_imag = jnp.einsum('fct,fcw->ftw', eff_real, imag_wide) - jnp.einsum('fct,fcw->ftw', eff_imag, real_wide)
        joined = jnp.concatenate([cross_real, cross_imag], axis=0)
        stacked = jnp.einsum('ftw,fn->twn', joined, inverse, precision=lax.Precision.HIGHEST)
        highest = lax.optimization_barrier(jnp.max(stacked, axis=2))
        return highest * scale / (templ_norm[:, None] * data_norm[None, :])
    real_blocks = jnp.transpose(templ_real.reshape(BAND_BINS, CHANNELS, count, block), (2, 0, 1, 3))
    imag_blocks = jnp.transpose(templ_imag.reshape(BAND_BINS, CHANNELS, count, block), (2, 0, 1, 3))
    mask_blocks = jnp.transpose(channel_mask.reshape(CHANNELS, count, block), (1, 0, 2))
    shift_blocks = jnp.transpose(moveout.reshape(CHANNELS, count, block), (1, 0, 2))
    peaks = lax.map(one_block, (real_blocks, imag_blocks, mask_blocks, shift_blocks))
    peak = peaks.reshape(TEMPLATES, WINDOWS)
    best = lax.optimization_barrier(jnp.max(peak, axis=0))
    return (peak, best)
```

```python
import functools
import math

import jax
import jax.numpy as jnp
import numpy as np
from jax import lax
from jax.experimental import pallas as pl
from jax.experimental.pallas import tpu as pltpu
from jax.sharding import PartitionSpec as P

FIRST_BIN = 16
TILE = 16

epsilon = 1e-06
VMEM_LIMIT = 62 * 1024 * 1024
MESH = pl.DeviceIdType.MESH


class Plan:
    def __init__(self, n, local, band, samples, templates, windows):
        self.n, self.local, self.band, self.samples = n, local, band, samples
        self.templates, self.windows = templates, windows
        self.block = math.gcd(windows, 128)
        self.blocks = windows // self.block
        self.pairs = band // 2
        self.groups = math.gcd(self.pairs, 4)
        self.per_group = self.pairs // self.groups
        self.chunks = self.blocks * self.groups
        self.layers = n // 4
        whole = local - local % 8
        self.order = (
            [(0, c) for c in range(whole)]
            + [(1, c) for c in range(whole)]
            + [(part, c) for part in range(2) for c in range(whole, local)]
        )
        count = len(self.order)
        self.full = count // TILE
        self.rest = count - self.full * TILE
        self.shared = 0 < self.rest <= 8
        self.tiles = self.full + (1 if self.rest else 0)
        self.rows = 2 * TILE * self.full + (0 if not self.rest else TILE if self.shared else 2 * TILE)
        self.depth = self.tiles * n * TILE
        self.pitch = 2 * band + 8
        self.row_pitch = self.rows + 8

    def row_of(self, parity, place):
        base = TILE * self.full
        if place < base:
            return parity * base + place
        if self.shared:
            return 2 * base + 8 * parity + place - base
        return 2 * base + TILE * parity + place - base

    def tile_row(self, parity, tile):
        if tile < self.full:
            return parity * TILE * self.full + tile * TILE
        return 2 * TILE * self.full + (0 if self.shared else TILE * parity)


def scan_kernel(
    plan, taps_ref, forward_ref, inverse_ref, mask_ref, move_ref, raw_ref, real_ref, imag_ref, peak_ref, best_ref,
    gathered, eff, cross, raw, table, wide, rows, real, imag, mask, move, cosine, sine, cos_step, sin_step, lined,
    square, energy, norm, mine, slots,
    raw_sem, side_sem, load_sem, recv_sem, mate_sem, send_sem, best_send, best_recv,
):
    n, layers, block, blocks = plan.n, plan.layers, plan.block, plan.blocks
    groups, per_group, chunks, pairs = plan.groups, plan.per_group, plan.chunks, plan.pairs
    band, templates, local, samples = plan.band, plan.templates, plan.local, plan.samples
    channels = n * local
    length = 2 * samples
    taps = taps_ref.shape[0]
    me = lax.axis_index("row")
    z, y, core = me // 4, lax.rem(me // 2, 2), lax.rem(me, 2)

    def index(z, y, core):
        return z * 4 + y * 2 + core

    partner = index(z, y, 1 - core)
    across = index(z, 1 - y, core)

    barrier = pltpu.get_barrier_semaphore()

    def greet(step, carry):
        pl.semaphore_signal(barrier, inc=1, device_id={"row": lax.rem(me + step, n)}, device_id_type=MESH)
        return carry

    lax.fori_loop(1, n, greet, 0)

    pieces = math.gcd(local, 4)
    per_piece = local // pieces

    def raw_load(i, p):
        slot = lax.rem(i, 2)
        return pltpu.make_async_copy(
            raw_ref.at[pl.ds(p * per_piece, per_piece), pl.ds(pl.multiple_of(i * block, block), block)],
            raw.at[slot, pl.ds(p * per_piece, per_piece)],
            raw_sem.at[slot, p],
        )

    def raw_start(i):
        for p in range(pieces):
            raw_load(i, p).start()

    def template_loads(g):
        bins = pl.ds(g * 2 * per_group, 2 * per_group)
        return [
            pltpu.make_async_copy(real_ref.at[bins], real.at[bins], load_sem.at[0, g]),
            pltpu.make_async_copy(imag_ref.at[bins], imag.at[bins], load_sem.at[1, g]),
        ]

    side_loads = [
        pltpu.make_async_copy(mask_ref, mask, side_sem.at[0]),
        pltpu.make_async_copy(move_ref, move, side_sem.at[1]),
    ]
    raw_start(0)
    if blocks > 1:
        raw_start(1)
    for copy in side_loads:
        copy.start()
    for g in range(groups):
        for copy in template_loads(g):
            copy.start()

    lane = lax.broadcasted_iota(jnp.int32, (8, 128), 1)
    low_half = lane < 2 * band
    total = jnp.zeros((samples, 128), jnp.float32)
    for i in range((taps + 1) // 2):
        odd = taps_ref[2 * i + 1] if 2 * i + 1 < taps else 0.0
        factor = jnp.where(low_half, taps_ref[2 * i], odd)[:1]
        total = total + factor * forward_ref[pl.ds(i, samples), :]
    high = total.astype(jnp.bfloat16).astype(jnp.float32)
    low = total - high
    half = low_half[:1]
    wide[pl.ds(0, samples, stride=2), :] = jnp.where(half, high, pltpu.roll(low, 2 * band, 1))
    wide[pl.ds(1, samples, stride=2), :] = jnp.where(half, pltpu.roll(high, 2 * band, 1), low)
    table[...] = wide[...].astype(jnp.bfloat16)
    if plan.rows * pairs != 2 * local * band:
        rows[...] = jnp.zeros_like(rows)

    def chunk(k, origin):
        i, g = k // groups, lax.rem(k, groups)
        return gathered.at[i, origin, pl.ds(g * per_group, per_group)]

    def send(k, zo, yo, target, slot):
        ref = chunk(k, index(zo, yo, core))
        return pltpu.make_async_remote_copy(
            src_ref=ref, dst_ref=ref, send_sem=send_sem.at[slot], recv_sem=recv_sem.at[k, zo * 2 + yo],
            device_id={"row": target}, device_id_type=MESH,
        )

    def give(k, zo, yo, slot):
        ref = chunk(k, index(zo, yo, core))
        return pltpu.make_async_remote_copy(
            src_ref=ref, dst_ref=ref, send_sem=send_sem.at[slot], recv_sem=mate_sem.at[k],
            device_id={"row": partner}, device_id_type=MESH,
        )

    def arrived(k, zo, yo):
        send(k, zo, yo, partner, 0).wait_recv()

    near = layers == 4 and groups % 2 == 0
    sent = []

    def slot_of(condition=None, share=1):
        sent.append((condition, share))
        return len(sent) - 1

    def when(condition, action):
        if condition is None:
            action()
        else:
            pl.when(condition)(action)

    first, second = [], []
    if near:
        far = z >= 2
        depth_of = jnp.where(far, 3 - z, z)
        inner, outer = depth_of == 1, depth_of == 0

        def at(q):
            return jnp.where(far, 3 - q, q)

        beside = 1 - depth_of
        own_slots = [(at(beside), None, slot_of()), (at(2), None, slot_of()), (at(3), inner, slot_of(inner))]
        own_across, own_mate = slot_of(), slot_of()
        line_over = [slot_of(outer, 2), slot_of(), slot_of()]
        line_on = slot_of(inner)
        line_mate = [slot_of() for _ in range(3)]
        side_on_outer, side_on_inner = slot_of(outer), slot_of(inner, 2)
        side_mate = [slot_of() for _ in range(4)]

        def first_events(k):
            even = lax.rem(k, 2) == 0
            for place, q in enumerate((beside, 2, 3)):
                origin = at(q)
                arrived(k, origin, y)
                condition = outer & even if place == 0 else None
                when(condition, lambda: send(k, origin, y, across, line_over[place]).start())
                if place == 2:
                    when(inner, lambda: send(k, origin, y, index(at(0), y, core), line_on).start())
                give(k, origin, y, line_mate[place]).start()
            arrived(k, z, 1 - y)
            when(outer, lambda: send(k, z, 1 - y, index(at(1), y, core), side_on_outer).start())
            when(inner & jnp.logical_not(even), lambda: send(k, z, 1 - y, index(at(0), y, core), side_on_inner).start())
            give(k, z, 1 - y, side_mate[0]).start()

        def second_events(k):
            for place, q in enumerate((beside, 2, 3)):
                origin = at(q)
                arrived(k, origin, 1 - y)
                give(k, origin, 1 - y, side_mate[1 + place]).start()
    else:
        offsets = range(1, layers)
        own_slots = [(lax.rem(z + s, layers), None, slot_of()) for s in offsets]
        own_across, own_mate = slot_of(), slot_of()
        line_over = [slot_of() for _ in offsets]
        line_mate = [slot_of() for _ in offsets]
        side_mate = [slot_of() for _ in range(layers)]

        def first_events(k):
            for place, s in enumerate(offsets):
                origin = lax.rem(z + s, layers)
                arrived(k, origin, y)
                send(k, origin, y, across, line_over[place]).start()
                give(k, origin, y, line_mate[place]).start()

        def second_events(k):
            for s in range(layers):
                origin = lax.rem(z + s, layers)
                arrived(k, origin, 1 - y)
                give(k, origin, 1 - y, side_mate[s]).start()

    def front(i, carry):
        slot = lax.rem(i, 2)
        weights = table[...]
        for c in range(local):
            if c % per_piece == 0:
                raw_load(i, c // per_piece).wait()
            trace = raw[slot, c]
            upper = trace.astype(jnp.bfloat16)
            lower = (trace - upper.astype(jnp.float32)).astype(jnp.bfloat16)
            spectra = jnp.dot(
                jnp.concatenate([upper, lower], axis=0), weights, preferred_element_type=jnp.float32
            )
            turned = (spectra[:block] + spectra[block:]).T
            value = turned[: 2 * band] + turned[2 * band :]
            for part in range(2):
                place = plan.order.index((part, c))
                for parity in range(2):
                    at_row = part * band + parity * pairs
                    rows[pl.ds(plan.row_of(parity, place), pairs, stride=plan.row_pitch), :] = value[
                        at_row : at_row + pairs
                    ]

        @pl.when(i + 2 < blocks)
        def _():
            raw_start(i + 2)

        for g in range(pairs):
            gathered[i, me, g] = rows[g * plan.row_pitch : g * plan.row_pitch + plan.rows, :].astype(jnp.bfloat16)

        @pl.when(i == 0)
        def _():
            pl.semaphore_wait(barrier, n - 1)

        for g in range(groups):
            k = i * groups + g
            send(k, z, y, across, own_across).start()
            for target, condition, number in own_slots:
                when(condition, lambda: send(k, z, y, index(target, y, core), number).start())
            give(k, z, y, own_mate).start()
        return carry

    lax.fori_loop(0, blocks, front, 0)

    for copy in side_loads:
        copy.wait()
    turn = 2.0 * math.pi / samples
    shift = move[...]
    weight = mask[...].astype(jnp.float32)
    phase = turn * lax.rem(FIRST_BIN * shift, samples).astype(jnp.float32)
    cosine[...] = weight * jnp.cos(phase)
    sine[...] = weight * jnp.sin(phase)
    phase = turn * shift.astype(jnp.float32)
    cos_step[...] = jnp.cos(phase)
    sin_step[...] = jnp.sin(phase)
    square[...] = jnp.zeros_like(square)
    energy[...] = jnp.zeros_like(energy)
    lined[...] = jnp.zeros_like(lined)
    mine[...] = jnp.zeros_like(mine)

    sub = lax.broadcasted_iota(jnp.int32, (8, templates), 0)

    def eight(origin, start, swap):
        wanted = plan.order[start : start + 8]
        result = None
        at_row = 0
        while at_row < 8:
            if at_row >= len(wanted):
                piece = jnp.zeros((8, templates), jnp.float32)
                end = 8
            else:
                part, c = wanted[at_row]
                end = at_row
                while end < len(wanted) and wanted[end] == (part, c + end - at_row):
                    end += 1
                source = 1 - part if swap else part
                piece = lined[pl.ds(8 + source * channels + origin * local + c - at_row, 8), :]
                if swap and part == 0:
                    piece = -piece
            result = piece if result is None else jnp.where(sub < at_row, result, piece)
            at_row = end
        return result

    def prepare(f, parity):
        c, s = cosine[...], sine[...]
        a = real[f].astype(jnp.float32)
        b = imag[f].astype(jnp.float32)
        whole_real = (a * c + b * s).astype(jnp.bfloat16).astype(jnp.float32)
        whole_imag = (b * c - a * s).astype(jnp.bfloat16).astype(jnp.float32)
        power = whole_real * whole_real + whole_imag * whole_imag
        square[...] += jnp.sum(power.reshape(channels // 8, 8, templates), axis=0)
        lined[pl.ds(8, channels), :] = whole_real
        lined[pl.ds(8 + channels, channels), :] = whole_imag
        c1, s1 = cos_step[...], sin_step[...]
        cosine[...] = c * c1 - s * s1
        sine[...] = s * c1 + c * s1
        blank = jnp.zeros((8, templates), jnp.float32)
        for side in range(2):
            for tile in range(plan.tiles):
                parts = []
                for origin in range(n):
                    if tile < plan.full or not plan.shared:
                        pair = [eight(origin, tile * TILE, side == 1), eight(origin, tile * TILE + 8, side == 1)]
                    else:
                        pair = [blank, blank]
                        pair[parity] = eight(origin, tile * TILE, side == 1)
                    parts += pair
                turned = jnp.concatenate(parts, axis=0).astype(jnp.bfloat16).T
                eff[f, side * templates : (side + 1) * templates, tile * n * TILE : (tile + 1) * n * TILE] = turned

    def prepare_group(g):
        for copy in template_loads(g):
            copy.wait()

        def one(p, carry):
            for parity in range(2):
                prepare(2 * p + parity, parity)
            return carry

        lax.fori_loop(g * per_group, (g + 1) * per_group, one, 0)

    def cross_chunk(k):
        i, g = k // groups, lax.rem(k, groups)
        slot = lax.rem(i, 2)
        mates = gathered.at[i, pl.ds(0, n // 2), pl.ds(g * per_group, per_group)]
        pltpu.make_async_copy(mates, mates, mate_sem.at[k]).wait()

        def one(p, carry):
            tiles = {}

            def load(row):
                if row not in tiles:
                    tiles[row] = gathered[i, :, p, row : row + TILE, :].reshape(n * TILE, block)
                return tiles[row]

            for parity in range(2):
                f = 2 * p + parity
                spec = jnp.concatenate([load(plan.tile_row(parity, tile)) for tile in range(plan.tiles)], axis=0)
                both = jnp.dot(eff[f], spec, preferred_element_type=jnp.float32)
                cross[slot, pl.ds(f, templates, stride=plan.pitch), :] = both[:templates]
                cross[slot, pl.ds(band + f, templates, stride=plan.pitch), :] = both[templates:]
            power = jnp.zeros((8, block), jnp.float32)
            for tile in tiles.values():
                value = tile.astype(jnp.float32)
                power += jnp.sum((value * value).reshape(n * TILE // 8, 8, block), axis=0)
            energy[i] += power
            return carry

        lax.fori_loop(g * per_group, (g + 1) * per_group, one, 0)

    scale = math.sqrt(2.0 * channels * band)
    octets = templates // 8 // groups

    def peak_part(q):
        i, part = q // groups, lax.rem(q, groups)
        slot = lax.rem(i, 2)
        inverse = inverse_ref[...]
        data_norm = jnp.sqrt(jnp.sum(energy[i], axis=0, keepdims=True) + epsilon)

        def octet(j, carry):
            found = []
            for t in range(0, 8, 2):
                joined = jnp.concatenate(
                    [
                        cross[slot, pl.ds(pl.multiple_of((j * 8 + t + u) * plan.pitch, 8), 2 * band), :]
                        for u in range(2)
                    ],
                    axis=1,
                )
                upper = joined.astype(jnp.bfloat16)
                lower = (joined - upper.astype(jnp.float32)).astype(jnp.bfloat16)
                stacked = jnp.dot(
                    inverse, jnp.concatenate([upper, lower, upper], axis=0), preferred_element_type=jnp.float32
                )
                top = jnp.max(stacked, axis=0, keepdims=True)
                found += [top[:, :block], top[:, block:]]
            here = pl.ds(pl.multiple_of(j * 8, 8), 8)
            value = jnp.concatenate(found, axis=0) * scale / (norm[here, :] * data_norm)
            peak_ref[here, pl.ds(pl.multiple_of(i * block, block), block)] = value
            return jnp.maximum(carry, value)

        lowest = jnp.full((8, block), -jnp.inf, jnp.float32)
        largest = lax.fori_loop(part * octets, (part + 1) * octets, octet, lowest)
        largest = jnp.max(largest, axis=0, keepdims=True)
        row = pl.ds(i, 1)
        mine[row, :] = jnp.where(part == 0, largest, jnp.maximum(mine[row, :], largest))

    def step(k, carry):
        @pl.when(k < groups)
        def _():
            prepare_group(k)

        @pl.when(k == groups)
        def _():
            total = jnp.sum(square[...], axis=0, keepdims=True)
            norm[...] = jnp.broadcast_to(jnp.sqrt(total + epsilon), (block, templates)).T

        @pl.when(k >= 2)
        def _():
            cross_chunk(k - 2)

        @pl.when(k >= 1 + groups)
        def _():
            peak_part(k - 1 - groups)

        @pl.when(k < chunks)
        def _():
            first_events(k)

        @pl.when((k >= 1) & (k <= chunks))
        def _():
            second_events(k - 1)

        return carry

    lax.fori_loop(0, chunks + 2, step, 0)

    def last(q, carry):
        peak_part(q)
        return carry

    lax.fori_loop(chunks + 1 - groups, chunks, last, 0)

    def best_copy(step):
        return pltpu.make_async_remote_copy(
            src_ref=mine, dst_ref=slots.at[step - 1], send_sem=best_send.at[0], recv_sem=best_recv.at[0],
            device_id={"row": lax.rem(me + step, n)}, device_id_type=MESH,
        )

    def best_start(step, carry):
        best_copy(step).start()
        return carry

    lax.fori_loop(1, n, best_start, 0)
    for number, (condition, share) in enumerate(sent):
        ref = gathered.at[:, 0] if share == 1 else gathered.at[:, 0, pl.ds(0, pairs // share)]
        wait = pltpu.make_async_remote_copy(
            src_ref=ref, dst_ref=ref, send_sem=send_sem.at[number], recv_sem=recv_sem.at[0, 0],
            device_id={"row": partner}, device_id_type=MESH,
        )
        when(condition, wait.wait_send)
    everyone = slots.at[pl.ds(0, n - 1)]
    all_best = pltpu.make_async_remote_copy(
        src_ref=everyone, dst_ref=everyone, send_sem=best_send.at[0], recv_sem=best_recv.at[0],
        device_id={"row": partner}, device_id_type=MESH,
    )
    all_best.wait()
    best_ref[...] = jnp.maximum(mine[...], jnp.max(slots[...], axis=0))


def send_slots(plan):
    if plan.layers == 4 and plan.groups % 2 == 0:
        return 18
    return 4 * plan.layers - 1


def body(n, raw_trace, fir_taps, templ_real, templ_imag, channel_mask, moveout):
    local, windows, length = raw_trace.shape
    samples = length // 2
    band, channels, templates = templ_real.shape
    plan = Plan(n, local, band, samples, templates, windows)
    bins = FIRST_BIN + np.arange(band)
    lags = np.arange(samples)
    angle = 2.0 * np.pi / samples * (bins[:, None] * lags[None, :] % samples)
    inverse = np.concatenate([np.cos(angle), -np.sin(angle)], axis=0)

    span = (fir_taps.shape[0] + 1) // 2
    forward = np.zeros((samples + span + 1, 2 * band))
    forward[:samples] = np.concatenate([inverse[:band][::2], inverse[:band][1::2], inverse[band:][::2], inverse[band:][1::2]]).T
    padded = -(-(samples + span) // 8) * 8
    both = np.zeros((padded, 4 * band), np.float32)
    both[: samples + span, : 2 * band] = forward[:-1]
    both[: samples + span, 2 * band :] = forward[1:]
    forward = jnp.asarray(both)

    inverse = inverse.T.astype(np.float32)
    high = inverse.astype(jnp.bfloat16)
    low = (inverse - high.astype(np.float32)).astype(jnp.bfloat16)
    inverse3 = jnp.asarray(np.concatenate([high, high, low], axis=1))

    vmem = pl.BlockSpec(memory_space=pltpu.VMEM)
    anywhere = pl.BlockSpec(memory_space=pl.ANY)
    f32, bf16 = jnp.float32, jnp.bfloat16
    pieces = math.gcd(local, 4)
    best_rows = -(-plan.blocks // 8) * 8
    peak, best = pl.pallas_call(
        functools.partial(scan_kernel, plan),
        out_shape=(
            jax.ShapeDtypeStruct((templates, windows), f32),
            jax.ShapeDtypeStruct((best_rows, plan.block), f32),
        ),
        in_specs=[pl.BlockSpec(memory_space=pltpu.SMEM), vmem, vmem] + [anywhere] * 5,
        out_specs=(vmem, vmem),
        scratch_shapes=[
            pltpu.VMEM((plan.blocks, n, plan.pairs, plan.rows, plan.block), bf16),
            pltpu.VMEM((band, 2 * templates, plan.depth), bf16),
            pltpu.VMEM((2, templates * plan.pitch, plan.block), f32),
            pltpu.VMEM((2, local, plan.block, length), f32),
            pltpu.VMEM((length, 4 * band), bf16),
            pltpu.VMEM((length, 4 * band), f32),
            pltpu.VMEM((plan.pairs * plan.row_pitch, plan.block), f32),
            pltpu.VMEM((band, channels, templates), bf16),
            pltpu.VMEM((band, channels, templates), bf16),
            pltpu.VMEM((channels, templates), jnp.int32),
            pltpu.VMEM((channels, templates), jnp.int32),
            pltpu.VMEM((channels, templates), f32),
            pltpu.VMEM((channels, templates), f32),
            pltpu.VMEM((channels, templates), f32),
            pltpu.VMEM((channels, templates), f32),
            pltpu.VMEM((2 * channels + 16, templates), f32),
            pltpu.VMEM((8, templates), f32),
            pltpu.VMEM((plan.blocks, 8, plan.block), f32),
            pltpu.VMEM((templates, plan.block), f32),
            pltpu.VMEM((best_rows, plan.block), f32),
            pltpu.VMEM((n - 1, best_rows, plan.block), f32),
            pltpu.SemaphoreType.DMA((2, pieces)),
            pltpu.SemaphoreType.DMA((2,)),
            pltpu.SemaphoreType.DMA((2, plan.groups)),
            pltpu.SemaphoreType.DMA((plan.chunks, n // 2)),
            pltpu.SemaphoreType.DMA((plan.chunks,)),
            pltpu.SemaphoreType.DMA((send_slots(plan),)),
            pltpu.SemaphoreType.DMA((1,)),
            pltpu.SemaphoreType.DMA((1,)),
        ],
        compiler_params=pltpu.CompilerParams(
            collective_id=0, has_side_effects=True, vmem_limit_bytes=VMEM_LIMIT
        ),
        name="gather_scan",
    )(fir_taps, forward, inverse3, channel_mask, moveout, raw_trace, templ_real, templ_imag)
    return (peak, best[: plan.blocks].reshape(windows))


def solution(mesh):
    in_specs = (
        P("row", "parts", None),
        P(),
        P(None, None, "row"),
        P(None, None, "row"),
        P(None, "row"),
        P(None, "row"),
    )
    out_specs = (P("row", "parts"), P("parts"))
    return jax.shard_map(
        functools.partial(body, mesh.shape["row"]),
        mesh=mesh,
        in_specs=in_specs,
        out_specs=out_specs,
        check_vma=False,
    )
```

```python
import functools
import math

import jax
import jax.numpy as jnp
import numpy as np
from jax import lax
from jax.experimental import pallas as pl
from jax.experimental.pallas import tpu as pltpu
from jax.sharding import PartitionSpec as P

FIRST_BIN = 16
TILE = 16
AHEAD = 3
CROSS_UNROLL = 4
PEAK_UNROLL = 4
LAG = 2
CROSS = 2 * LAG + 1
ORDER = ("norm", "own", "direct", "second", "third", "cross", "peak", "prepare")
LATE = ("third", "cross", "peak", "second")

epsilon = 1e-06
VMEM_LIMIT = 62 * 1024 * 1024
MESH = pl.DeviceIdType.MESH


class Plan:
    def __init__(self, n, local, band, samples, templates, windows):
        self.n, self.local, self.band, self.samples = n, local, band, samples
        self.templates, self.windows = templates, windows
        self.block = math.gcd(windows, 128)
        self.blocks = windows // self.block
        self.pairs = band // 2
        self.groups = math.gcd(self.pairs, 4)
        self.per_group = self.pairs // self.groups
        self.chunks = self.blocks * self.groups
        self.layers = n // 4
        whole = local - local % 8
        self.order = (
            [(0, c) for c in range(whole)]
            + [(1, c) for c in range(whole)]
            + [(part, c) for part in range(2) for c in range(whole, local)]
        )
        count = len(self.order)
        self.full = count // TILE
        self.rest = count - self.full * TILE
        self.shared = 0 < self.rest <= 8
        self.tiles = self.full + (1 if self.rest else 0)
        self.rows = 2 * TILE * self.full + (0 if not self.rest else TILE if self.shared else 2 * TILE)
        self.depth = self.tiles * n * TILE
        self.pitch = 2 * band + 8
        self.row_pitch = self.rows + 8

    def row_of(self, parity, place):
        base = TILE * self.full
        if place < base:
            return parity * base + place
        if self.shared:
            return 2 * base + 8 * parity + place - base
        return 2 * base + TILE * parity + place - base

    def tile_row(self, parity, tile):
        if tile < self.full:
            return parity * TILE * self.full + tile * TILE
        return 2 * TILE * self.full + (0 if self.shared else TILE * parity)


def scan_kernel(
    plan, taps_ref, forward_ref, inverse_ref, mask_ref, move_ref, raw_ref, real_ref, imag_ref, peak_ref, best_ref,
    gathered, eff, cross, raw, table, wide, rows, real, imag, mask, move, cosine, sine, cos_step, sin_step, lined,
    square, energy, norm, tops, mine, slots,
    raw_sem, side_sem, load_sem, recv_sem, mate_sem, give_sem, send_sem, best_send, best_recv,
):
    n, layers, block, blocks = plan.n, plan.layers, plan.block, plan.blocks
    groups, per_group, chunks, pairs = plan.groups, plan.per_group, plan.chunks, plan.pairs
    band, templates, local, samples = plan.band, plan.templates, plan.local, plan.samples
    channels = n * local
    length = 2 * samples
    taps = taps_ref.shape[0]
    me = lax.axis_index("row")
    z, y, core = me // 4, lax.rem(me // 2, 2), lax.rem(me, 2)

    def index(z, y, core):
        return z * 4 + y * 2 + core

    partner = index(z, y, 1 - core)
    across = index(z, 1 - y, core)

    def spread(begin, count, unroll, action, value):
        unroll = math.gcd(count, unroll)

        def several(j, carry):
            for u in range(unroll):
                carry = action(begin + j * unroll + u, carry)
            return carry

        return several(0, value) if unroll == count else lax.fori_loop(0, count // unroll, several, value)

    barrier = pltpu.get_barrier_semaphore()

    def greet(step, carry):
        pl.semaphore_signal(barrier, inc=1, device_id={"row": lax.rem(me + step, n)}, device_id_type=MESH)
        return carry

    lax.fori_loop(1, n, greet, 0)

    pieces = math.gcd(local, 4)
    per_piece = local // pieces

    def raw_load(i, p):
        slot = lax.rem(i, 2)
        return pltpu.make_async_copy(
            raw_ref.at[pl.ds(p * per_piece, per_piece), pl.ds(pl.multiple_of(i * block, block), block)],
            raw.at[slot, pl.ds(p * per_piece, per_piece)],
            raw_sem.at[slot, p],
        )

    def raw_start(i):
        for p in range(pieces):
            raw_load(i, p).start()

    def template_loads(g):
        bins = pl.ds(g * 2 * per_group, 2 * per_group)
        return [
            pltpu.make_async_copy(real_ref.at[bins], real.at[bins], load_sem.at[0, g]),
            pltpu.make_async_copy(imag_ref.at[bins], imag.at[bins], load_sem.at[1, g]),
        ]

    side_loads = [
        pltpu.make_async_copy(mask_ref, mask, side_sem.at[0]),
        pltpu.make_async_copy(move_ref, move, side_sem.at[1]),
    ]
    raw_start(0)
    if blocks > 1:
        raw_start(1)
    for copy in side_loads:
        copy.start()
    for g in range(groups):
        for copy in template_loads(g):
            copy.start()

    lane = lax.broadcasted_iota(jnp.int32, (8, 128), 1)
    low_half = lane < 2 * band
    total = jnp.zeros((samples, 128), jnp.float32)
    for i in range((taps + 1) // 2):
        odd = taps_ref[2 * i + 1] if 2 * i + 1 < taps else 0.0
        factor = jnp.where(low_half, taps_ref[2 * i], odd)[:1]
        total = total + factor * forward_ref[pl.ds(i, samples), :]
    high = total.astype(jnp.bfloat16).astype(jnp.float32)
    low = total - high
    half = low_half[:1]
    wide[pl.ds(0, samples, stride=2), :] = jnp.where(half, high, pltpu.roll(low, 2 * band, 1))
    wide[pl.ds(1, samples, stride=2), :] = jnp.where(half, pltpu.roll(high, 2 * band, 1), low)
    table[...] = wide[...].astype(jnp.bfloat16)
    if plan.rows * pairs != 2 * local * band:
        rows[...] = jnp.zeros_like(rows)

    def chunk(k, zo, yo):
        i, g = k // groups, lax.rem(k, groups)
        return gathered.at[i, core, zo * 2 + yo, pl.ds(g * per_group, per_group)]

    def shared_chunk(k, side):
        i, g = k // groups, lax.rem(k, groups)
        return gathered.at[i, side, :, pl.ds(g * per_group, per_group)]

    def send(k, zo, yo, target, slot):
        ref = chunk(k, zo, yo)
        return pltpu.make_async_remote_copy(
            src_ref=ref, dst_ref=ref, send_sem=send_sem.at[slot], recv_sem=recv_sem.at[k, zo * 2 + yo],
            device_id={"row": target}, device_id_type=MESH,
        )

    def give(k):
        ref = shared_chunk(k, core)
        return pltpu.make_async_remote_copy(
            src_ref=ref, dst_ref=ref, send_sem=give_sem.at[0], recv_sem=mate_sem.at[k],
            device_id={"row": partner}, device_id_type=MESH,
        )

    def arrived(k, zo, yo):
        send(k, zo, yo, partner, 0).wait_recv()

    near = layers == 4 and groups % 2 == 0
    sent = []

    def slot_of(condition=None, share=1):
        sent.append((condition, share))
        return len(sent) - 1

    def when(condition, action):
        if condition is None:
            action()
        else:
            pl.when(condition)(action)

    if near:
        far = z >= 2
        depth_of = jnp.where(far, 3 - z, z)
        inner, outer = depth_of == 1, depth_of == 0

        def at(q):
            return jnp.where(far, 3 - q, q)

        beside = 1 - depth_of
        own_slots = [(at(beside), None, slot_of()), (at(2), None, slot_of()), (at(3), inner, slot_of(inner))]
        own_across = slot_of()
        line_over = [slot_of(outer, 2), slot_of(), slot_of()]
        line_on = slot_of(inner)
        side_on_outer, side_on_inner = slot_of(outer), slot_of(inner, 2)

        def line_event(k, place, q):
            origin = at(q)
            arrived(k, origin, y)
            condition = outer & (lax.rem(k, 2) == 0) if place == 0 else None
            when(condition, lambda: send(k, origin, y, across, line_over[place]).start())
            if place == 2:
                when(inner, lambda: send(k, origin, y, index(at(0), y, core), line_on).start())

        def direct_events(k):
            line_event(k, 0, beside)
            line_event(k, 1, 2)
            pl.when(inner)(lambda: line_event(k, 2, 3))
            arrived(k, z, 1 - y)
            when(outer, lambda: send(k, z, 1 - y, index(at(1), y, core), side_on_outer).start())
            odd = inner & (lax.rem(k, 2) == 1)
            when(odd, lambda: send(k, z, 1 - y, index(at(0), y, core), side_on_inner).start())

        def second_events(k):
            pl.when(outer)(lambda: line_event(k, 2, 3))
            arrived(k, at(beside), 1 - y)
            arrived(k, at(2), 1 - y)

        def third_events(k):
            arrived(k, at(3), 1 - y)
            give(k).start()
    else:
        offsets = range(1, layers)
        own_slots = [(lax.rem(z + s, layers), None, slot_of()) for s in offsets]
        own_across = slot_of()
        line_over = [slot_of() for _ in offsets]

        def direct_events(k):
            for place, s in enumerate(offsets):
                origin = lax.rem(z + s, layers)
                arrived(k, origin, y)
                send(k, origin, y, across, line_over[place]).start()

        def second_events(k):
            for s in range(layers):
                origin = lax.rem(z + s, layers)
                arrived(k, origin, 1 - y)

        def third_events(k):
            give(k).start()

    def own_events(k):
        send(k, z, y, across, own_across).start()
        for target, condition, number in own_slots:
            when(condition, lambda: send(k, z, y, index(target, y, core), number).start())

    def front(i, carry):
        slot = lax.rem(i, 2)
        weights = table[...]
        for c in range(local):
            if c % per_piece == 0:
                raw_load(i, c // per_piece).wait()
            trace = raw[slot, c]
            upper = trace.astype(jnp.bfloat16)
            lower = (trace - upper.astype(jnp.float32)).astype(jnp.bfloat16)
            spectra = jnp.dot(
                jnp.concatenate([upper, lower], axis=0), weights, preferred_element_type=jnp.float32
            )
            turned = (spectra[:block] + spectra[block:]).T
            value = turned[: 2 * band] + turned[2 * band :]
            for part in range(2):
                place = plan.order.index((part, c))
                for parity in range(2):
                    at_row = part * band + parity * pairs
                    rows[pl.ds(plan.row_of(parity, place), pairs, stride=plan.row_pitch), :] = value[
                        at_row : at_row + pairs
                    ]

        @pl.when(i + 2 < blocks)
        def _():
            raw_start(i + 2)

        for g in range(pairs):
            gathered[i, core, me // 2, g] = rows[g * plan.row_pitch : g * plan.row_pitch + plan.rows, :].astype(jnp.bfloat16)

        @pl.when(i == 0)
        def _():
            pl.semaphore_wait(barrier, n - 1)

        for g in range(groups):
            k = i * groups + g
            pl.when(k < AHEAD)(lambda: own_events(k))
        return carry

    lax.fori_loop(0, blocks, front, 0)

    for copy in side_loads:
        copy.wait()
    turn = 2.0 * math.pi / samples
    shift = move[...]
    weight = mask[...].astype(jnp.float32)
    phase = turn * lax.rem(FIRST_BIN * shift, samples).astype(jnp.float32)
    cosine[...] = weight * jnp.cos(phase)
    sine[...] = weight * jnp.sin(phase)
    phase = turn * shift.astype(jnp.float32)
    cos_step[...] = jnp.cos(phase)
    sin_step[...] = jnp.sin(phase)
    square[...] = jnp.zeros_like(square)
    energy[...] = jnp.zeros_like(energy)
    lined[...] = jnp.zeros_like(lined)
    mine[...] = jnp.zeros_like(mine)

    sub = lax.broadcasted_iota(jnp.int32, (8, templates), 0)

    def eight(origin, start, swap):
        wanted = plan.order[start : start + 8]
        result = None
        at_row = 0
        while at_row < 8:
            if at_row >= len(wanted):
                piece = jnp.zeros((8, templates), jnp.float32)
                end = 8
            else:
                part, c = wanted[at_row]
                end = at_row
                while end < len(wanted) and wanted[end] == (part, c + end - at_row):
                    end += 1
                source = 1 - part if swap else part
                piece = lined[pl.ds(8 + source * channels + origin * local + c - at_row, 8), :]
                if swap and part == 0:
                    piece = -piece
            result = piece if result is None else jnp.where(sub < at_row, result, piece)
            at_row = end
        return result

    def prepare(f, parity):
        c, s = cosine[...], sine[...]
        a = real[f].astype(jnp.float32)
        b = imag[f].astype(jnp.float32)
        whole_real = (a * c + b * s).astype(jnp.bfloat16).astype(jnp.float32)
        whole_imag = (b * c - a * s).astype(jnp.bfloat16).astype(jnp.float32)
        power = whole_real * whole_real + whole_imag * whole_imag
        square[...] += jnp.sum(power.reshape(channels // 8, 8, templates), axis=0)
        lined[pl.ds(8, channels), :] = whole_real
        lined[pl.ds(8 + channels, channels), :] = whole_imag
        c1, s1 = cos_step[...], sin_step[...]
        cosine[...] = c * c1 - s * s1
        sine[...] = s * c1 + c * s1
        blank = jnp.zeros((8, templates), jnp.float32)
        for swap in range(2):
            for tile in range(plan.tiles):
                parts = []
                for origin in [chip * 2 + side for side in range(2) for chip in range(n // 2)]:
                    if tile < plan.full or not plan.shared:
                        pair = [eight(origin, tile * TILE, swap == 1), eight(origin, tile * TILE + 8, swap == 1)]
                    else:
                        pair = [blank, blank]
                        pair[parity] = eight(origin, tile * TILE, swap == 1)
                    parts += pair
                turned = jnp.concatenate(parts, axis=0).astype(jnp.bfloat16).T
                eff[f, swap * templates : (swap + 1) * templates, tile * n * TILE : (tile + 1) * n * TILE] = turned

    def prepare_group(g):
        for copy in template_loads(g):
            copy.wait()

        def one(p, carry):
            for parity in range(2):
                prepare(2 * p + parity, parity)
            return carry

        lax.fori_loop(g * per_group, (g + 1) * per_group, one, 0)

    def cross_chunk(k):
        i, g = k // groups, lax.rem(k, groups)
        slot = lax.rem(i, 2)
        mates = shared_chunk(k, 1 - core)
        pltpu.make_async_copy(mates, mates, mate_sem.at[k]).wait()

        def one(p, carry):
            tiles = {}

            def load(row):
                if row not in tiles:
                    tiles[row] = gathered[i, :, :, p, row : row + TILE, :].reshape(n * TILE, block)
                return tiles[row]

            for parity in range(2):
                f = 2 * p + parity
                spec = jnp.concatenate([load(plan.tile_row(parity, tile)) for tile in range(plan.tiles)], axis=0)
                both = jnp.dot(eff[f], spec, preferred_element_type=jnp.float32)
                cross[slot, pl.ds(f, templates, stride=plan.pitch), :] = both[:templates]
                cross[slot, pl.ds(band + f, templates, stride=plan.pitch), :] = both[templates:]
            power = jnp.zeros((8, block), jnp.float32)
            for tile in tiles.values():
                value = tile.astype(jnp.float32)
                power += jnp.sum((value * value).reshape(n * TILE // 8, 8, block), axis=0)
            energy[i] += power
            return carry

        spread(g * per_group, per_group, CROSS_UNROLL, one, 0)

    scale = math.sqrt(2.0 * channels * band)
    octets = templates // 8 // groups

    def peak_part(q):
        i, part = q // groups, lax.rem(q, groups)
        slot = lax.rem(i, 2)
        inverse = inverse_ref[...]
        data_norm = jnp.sqrt(jnp.sum(energy[i], axis=0, keepdims=True) + epsilon)

        def octet(j, carry):
            bank = lax.rem(j, 4)
            for t in range(0, 8, 2):
                joined = jnp.concatenate(
                    [
                        cross[slot, pl.ds(pl.multiple_of((j * 8 + t + u) * plan.pitch, 8), 2 * band), :]
                        for u in range(2)
                    ],
                    axis=1,
                )
                upper = joined.astype(jnp.bfloat16)
                lower = (joined - upper.astype(jnp.float32)).astype(jnp.bfloat16)
                stacked = jnp.dot(
                    inverse, jnp.concatenate([upper, lower, upper], axis=0), preferred_element_type=jnp.float32
                )
                top = jnp.max(stacked.reshape(samples // 8, 8, 2 * block), axis=0)
                tops[bank, 8 * t : 8 * t + 8, :] = top[:, :block]
                tops[bank, 8 * t + 8 : 8 * t + 16, :] = top[:, block:]
            here = pl.ds(pl.multiple_of(j * 8, 8), 8)
            value = tops[bank, pl.ds(0, 8, stride=8), :]
            for s in range(1, 8):
                value = jnp.maximum(value, tops[bank, pl.ds(s, 8, stride=8), :])
            value = value * scale / (norm[here, :] * data_norm)
            peak_ref[here, pl.ds(pl.multiple_of(i * block, block), block)] = value
            return jnp.maximum(carry, value)

        lowest = jnp.full((8, block), -jnp.inf, jnp.float32)
        largest = spread(part * octets, octets, PEAK_UNROLL, octet, lowest)
        largest = jnp.max(largest, axis=0, keepdims=True)
        row = pl.ds(i, 1)
        mine[row, :] = jnp.where(part == 0, largest, jnp.maximum(mine[row, :], largest))

    def step(order, k, carry):
        def guarded(condition, action, index):
            pl.when(condition)(lambda: action(index))

        def finish_norm(k):
            total = jnp.sum(square[...], axis=0, keepdims=True)
            norm[...] = jnp.broadcast_to(jnp.sqrt(total + epsilon), (block, templates)).T

        peak_lag = CROSS + groups - 1
        work = {
            "cross": (k >= CROSS, cross_chunk, k - CROSS),
            "peak": (k >= peak_lag, peak_part, k - peak_lag),
            "own": (k + AHEAD < chunks, own_events, k + AHEAD),
            "direct": (k < chunks, direct_events, k),
            "second": ((k >= LAG) & (k < chunks + LAG), second_events, k - LAG),
            "third": ((k >= 2 * LAG) & (k < chunks + 2 * LAG), third_events, k - 2 * LAG),
            "prepare": (k < groups, prepare_group, k),
            "norm": (k == groups, finish_norm, k),
        }
        for name in order:
            guarded(*work[name])
        return carry

    lax.fori_loop(0, chunks, functools.partial(step, ORDER), 0)
    lax.fori_loop(chunks, chunks + CROSS, functools.partial(step, LATE), 0)

    def last(q, carry):
        peak_part(q)
        return carry

    lax.fori_loop(chunks + 1 - groups, chunks, last, 0)

    def best_copy(step):
        return pltpu.make_async_remote_copy(
            src_ref=mine, dst_ref=slots.at[step - 1], send_sem=best_send.at[0], recv_sem=best_recv.at[0],
            device_id={"row": lax.rem(me + step, n)}, device_id_type=MESH,
        )

    def best_start(step, carry):
        best_copy(step).start()
        return carry

    lax.fori_loop(1, n, best_start, 0)
    for number, (condition, share) in enumerate(sent):
        ref = gathered.at[:, 0, 0] if share == 1 else gathered.at[:, 0, 0, pl.ds(0, pairs // share)]
        wait = pltpu.make_async_remote_copy(
            src_ref=ref, dst_ref=ref, send_sem=send_sem.at[number], recv_sem=recv_sem.at[0, 0],
            device_id={"row": partner}, device_id_type=MESH,
        )
        when(condition, wait.wait_send)
    whole = gathered.at[:, 0]
    pltpu.make_async_remote_copy(
        src_ref=whole, dst_ref=whole, send_sem=give_sem.at[0], recv_sem=recv_sem.at[0, 0],
        device_id={"row": partner}, device_id_type=MESH,
    ).wait_send()
    everyone = slots.at[pl.ds(0, n - 1)]
    all_best = pltpu.make_async_remote_copy(
        src_ref=everyone, dst_ref=everyone, send_sem=best_send.at[0], recv_sem=best_recv.at[0],
        device_id={"row": partner}, device_id_type=MESH,
    )
    all_best.wait()
    best_ref[...] = jnp.maximum(mine[...], jnp.max(slots[...], axis=0))


def send_slots(plan):
    if plan.layers == 4 and plan.groups % 2 == 0:
        return 10
    return 2 * plan.layers - 1


def body(n, raw_trace, fir_taps, templ_real, templ_imag, channel_mask, moveout):
    local, windows, length = raw_trace.shape
    samples = length // 2
    band, channels, templates = templ_real.shape
    plan = Plan(n, local, band, samples, templates, windows)
    bins = FIRST_BIN + np.arange(band)
    lags = np.arange(samples)
    angle = 2.0 * np.pi / samples * (bins[:, None] * lags[None, :] % samples)
    inverse = np.concatenate([np.cos(angle), -np.sin(angle)], axis=0)

    span = (fir_taps.shape[0] + 1) // 2
    forward = np.zeros((samples + span + 1, 2 * band))
    forward[:samples] = np.concatenate([inverse[:band][::2], inverse[:band][1::2], inverse[band:][::2], inverse[band:][1::2]]).T
    padded = -(-(samples + span) // 8) * 8
    both = np.zeros((padded, 4 * band), np.float32)
    both[: samples + span, : 2 * band] = forward[:-1]
    both[: samples + span, 2 * band :] = forward[1:]
    forward = jnp.asarray(both)

    inverse = inverse.T.astype(np.float32)
    high = inverse.astype(jnp.bfloat16)
    low = (inverse - high.astype(np.float32)).astype(jnp.bfloat16)
    inverse3 = jnp.asarray(np.concatenate([high, high, low], axis=1))

    vmem = pl.BlockSpec(memory_space=pltpu.VMEM)
    anywhere = pl.BlockSpec(memory_space=pl.ANY)
    f32, bf16 = jnp.float32, jnp.bfloat16
    pieces = math.gcd(local, 4)
    best_rows = -(-plan.blocks // 8) * 8
    peak, best = pl.pallas_call(
        functools.partial(scan_kernel, plan),
        out_shape=(
            jax.ShapeDtypeStruct((templates, windows), f32),
            jax.ShapeDtypeStruct((best_rows, plan.block), f32),
        ),
        in_specs=[pl.BlockSpec(memory_space=pltpu.SMEM), vmem, vmem] + [anywhere] * 5,
        out_specs=(vmem, vmem),
        scratch_shapes=[
            pltpu.VMEM((plan.blocks, 2, n // 2, plan.pairs, plan.rows, plan.block), bf16),
            pltpu.VMEM((band, 2 * templates, plan.depth), bf16),
            pltpu.VMEM((2, templates * plan.pitch, plan.block), f32),
            pltpu.VMEM((2, local, plan.block, length), f32),
            pltpu.VMEM((length, 4 * band), bf16),
            pltpu.VMEM((length, 4 * band), f32),
            pltpu.VMEM((plan.pairs * plan.row_pitch, plan.block), f32),
            pltpu.VMEM((band, channels, templates), bf16),
            pltpu.VMEM((band, channels, templates), bf16),
            pltpu.VMEM((channels, templates), jnp.int32),
            pltpu.VMEM((channels, templates), jnp.int32),
            pltpu.VMEM((channels, templates), f32),
            pltpu.VMEM((channels, templates), f32),
            pltpu.VMEM((channels, templates), f32),
            pltpu.VMEM((channels, templates), f32),
            pltpu.VMEM((2 * channels + 16, templates), f32),
            pltpu.VMEM((8, templates), f32),
            pltpu.VMEM((plan.blocks, 8, plan.block), f32),
            pltpu.VMEM((templates, plan.block), f32),
            pltpu.VMEM((4, 64, plan.block), f32),
            pltpu.VMEM((best_rows, plan.block), f32),
            pltpu.VMEM((n - 1, best_rows, plan.block), f32),
            pltpu.SemaphoreType.DMA((2, pieces)),
            pltpu.SemaphoreType.DMA((2,)),
            pltpu.SemaphoreType.DMA((2, plan.groups)),
            pltpu.SemaphoreType.DMA((plan.chunks, n // 2)),
            pltpu.SemaphoreType.DMA((plan.chunks,)),
            pltpu.SemaphoreType.DMA((1,)),
            pltpu.SemaphoreType.DMA((send_slots(plan),)),
            pltpu.SemaphoreType.DMA((1,)),
            pltpu.SemaphoreType.DMA((1,)),
        ],
        compiler_params=pltpu.CompilerParams(
            collective_id=0, has_side_effects=True, vmem_limit_bytes=VMEM_LIMIT
        ),
        name="gather_scan",
    )(fir_taps, forward, inverse3, channel_mask, moveout, raw_trace, templ_real, templ_imag)
    return (peak, best[: plan.blocks].reshape(windows))


def solution(mesh):
    in_specs = (
        P("row", "parts", None),
        P(),
        P(None, None, "row"),
        P(None, None, "row"),
        P(None, "row"),
        P(None, "row"),
    )
    out_specs = (P("row", "parts"), P("parts"))
    return jax.shard_map(
        functools.partial(body, mesh.shape["row"]),
        mesh=mesh,
        in_specs=in_specs,
        out_specs=out_specs,
        check_vma=False,
    )
```

```python
import functools
import math

import jax
import jax.numpy as jnp
import numpy as np
from jax import lax
from jax.experimental import pallas as pl
from jax.experimental.pallas import tpu as pltpu
from jax.sharding import PartitionSpec as P

FIRST_BIN = 16
TILE = 16
AHEAD = 3
CROSS_UNROLL = 4
PEAK_UNROLL = 4
LAG = 2
CROSS = 2 * LAG + 1
ORDER = ("norm", "own", "direct", "second", "third", "cross", "peak", "prepare")
LATE = ("third", "cross", "peak", "second")

epsilon = 1e-06
VMEM_LIMIT = 62 * 1024 * 1024
MESH = pl.DeviceIdType.MESH


class Plan:
    def __init__(self, n, local, band, samples, templates, windows):
        self.n, self.local, self.band, self.samples = n, local, band, samples
        self.templates, self.windows = templates, windows
        self.block = math.gcd(windows, 128)
        self.blocks = windows // self.block
        self.pairs = band // 2
        self.groups = math.gcd(self.pairs, 4)
        self.per_group = self.pairs // self.groups
        self.chunks = self.blocks * self.groups
        self.layers = n // 4
        whole = local - local % 8
        self.order = (
            [(0, c) for c in range(whole)]
            + [(1, c) for c in range(whole)]
            + [(part, c) for part in range(2) for c in range(whole, local)]
        )
        count = len(self.order)
        self.full = count // TILE
        self.rest = count - self.full * TILE
        self.shared = 0 < self.rest <= 8
        self.tiles = self.full + (1 if self.rest else 0)
        self.rows = 2 * TILE * self.full + (0 if not self.rest else TILE if self.shared else 2 * TILE)
        self.depth = self.tiles * n * TILE
        self.pitch = 2 * band + 8
        self.row_pitch = self.rows + 8

    def row_of(self, parity, place):
        base = TILE * self.full
        if place < base:
            return parity * base + place
        if self.shared:
            return 2 * base + 8 * parity + place - base
        return 2 * base + TILE * parity + place - base

    def tile_row(self, parity, tile):
        if tile < self.full:
            return parity * TILE * self.full + tile * TILE
        return 2 * TILE * self.full + (0 if self.shared else TILE * parity)


def scan_kernel(
    plan, taps_ref, forward_ref, inverse_ref, mask_ref, move_ref, raw_ref, real_ref, imag_ref, peak_ref, best_ref,
    gathered, eff, cross, raw, table, wide, rows, real, imag, mask, move, cosine, sine, cos_step, sin_step, lined,
    square, energy, norm, tops, mine, slots,
    raw_sem, side_sem, load_sem, recv_sem, mate_sem, give_sem, send_sem, best_send, best_recv,
):
    n, layers, block, blocks = plan.n, plan.layers, plan.block, plan.blocks
    groups, per_group, chunks, pairs = plan.groups, plan.per_group, plan.chunks, plan.pairs
    band, templates, local, samples = plan.band, plan.templates, plan.local, plan.samples
    channels = n * local
    length = 2 * samples
    taps = taps_ref.shape[0]
    me = lax.axis_index("row")
    z, y, core = me // 4, lax.rem(me // 2, 2), lax.rem(me, 2)

    def index(z, y, core):
        return z * 4 + y * 2 + core

    partner = index(z, y, 1 - core)
    across = index(z, 1 - y, core)

    def spread(begin, count, unroll, action, value):
        unroll = math.gcd(count, unroll)

        def several(j, carry):
            for u in range(unroll):
                carry = action(begin + j * unroll + u, carry)
            return carry

        return several(0, value) if unroll == count else lax.fori_loop(0, count // unroll, several, value)

    barrier = pltpu.get_barrier_semaphore()

    def greet(step, carry):
        pl.semaphore_signal(barrier, inc=1, device_id={"row": lax.rem(me + step, n)}, device_id_type=MESH)
        return carry

    lax.fori_loop(1, n, greet, 0)

    pieces = math.gcd(local, 4)
    per_piece = local // pieces

    def raw_load(i, p):
        slot = lax.rem(i, 2)
        return pltpu.make_async_copy(
            raw_ref.at[pl.ds(p * per_piece, per_piece), pl.ds(pl.multiple_of(i * block, block), block)],
            raw.at[slot, pl.ds(p * per_piece, per_piece)],
            raw_sem.at[slot, p],
        )

    def raw_start(i):
        for p in range(pieces):
            raw_load(i, p).start()

    def template_loads(g):
        bins = pl.ds(g * 2 * per_group, 2 * per_group)
        return [
            pltpu.make_async_copy(real_ref.at[bins], real.at[bins], load_sem.at[0, g]),
            pltpu.make_async_copy(imag_ref.at[bins], imag.at[bins], load_sem.at[1, g]),
        ]

    side_loads = [
        pltpu.make_async_copy(mask_ref, mask, side_sem.at[0]),
        pltpu.make_async_copy(move_ref, move, side_sem.at[1]),
    ]
    raw_start(0)
    if blocks > 1:
        raw_start(1)
    for copy in side_loads:
        copy.start()
    for g in range(groups):
        for copy in template_loads(g):
            copy.start()

    lane = lax.broadcasted_iota(jnp.int32, (8, 128), 1)
    low_half = lane < 2 * band
    total = jnp.zeros((samples, 128), jnp.float32)
    for i in range((taps + 1) // 2):
        odd = taps_ref[2 * i + 1] if 2 * i + 1 < taps else 0.0
        factor = jnp.where(low_half, taps_ref[2 * i], odd)[:1]
        total = total + factor * forward_ref[pl.ds(i, samples), :]
    high = total.astype(jnp.bfloat16).astype(jnp.float32)
    low = total - high
    half = low_half[:1]
    wide[pl.ds(0, samples, stride=2), :] = jnp.where(half, high, pltpu.roll(low, 2 * band, 1))
    wide[pl.ds(1, samples, stride=2), :] = jnp.where(half, pltpu.roll(high, 2 * band, 1), low)
    table[...] = wide[...].astype(jnp.bfloat16)
    if plan.rows * pairs != 2 * local * band:
        rows[...] = jnp.zeros_like(rows)

    def chunk(k, zo, yo):
        i, g = k // groups, lax.rem(k, groups)
        return gathered.at[i, core, zo * 2 + yo, pl.ds(g * per_group, per_group)]

    def shared_chunk(k, side):
        i, g = k // groups, lax.rem(k, groups)
        return gathered.at[i, side, :, pl.ds(g * per_group, per_group)]

    def send(k, zo, yo, target, slot):
        ref = chunk(k, zo, yo)
        return pltpu.make_async_remote_copy(
            src_ref=ref, dst_ref=ref, send_sem=send_sem.at[slot], recv_sem=recv_sem.at[k, zo * 2 + yo],
            device_id={"row": target}, device_id_type=MESH,
        )

    def give(k):
        ref = shared_chunk(k, core)
        return pltpu.make_async_remote_copy(
            src_ref=ref, dst_ref=ref, send_sem=give_sem.at[0], recv_sem=mate_sem.at[k],
            device_id={"row": partner}, device_id_type=MESH,
        )

    def arrived(k, zo, yo):
        send(k, zo, yo, partner, 0).wait_recv()

    near = layers == 4 and groups % 2 == 0
    sent = []

    def slot_of(condition=None, share=1):
        sent.append((condition, share))
        return len(sent) - 1

    def when(condition, action):
        if condition is None:
            action()
        else:
            pl.when(condition)(action)

    if near:
        far = z >= 2
        depth_of = jnp.where(far, 3 - z, z)
        inner, outer = depth_of == 1, depth_of == 0

        def at(q):
            return jnp.where(far, 3 - q, q)

        beside = 1 - depth_of
        own_slots = [(at(beside), None, slot_of()), (at(2), None, slot_of()), (at(3), inner, slot_of(inner))]
        own_across = slot_of()
        line_over = [slot_of(outer, 2), slot_of(), slot_of()]
        line_on = slot_of(inner)
        side_on_outer, side_on_inner = slot_of(outer), slot_of(inner, 2)

        def line_event(k, place, q):
            origin = at(q)
            arrived(k, origin, y)
            condition = outer & (lax.rem(k, 2) == 0) if place == 0 else None
            when(condition, lambda: send(k, origin, y, across, line_over[place]).start())
            if place == 2:
                when(inner, lambda: send(k, origin, y, index(at(0), y, core), line_on).start())

        def direct_events(k):
            line_event(k, 0, beside)
            line_event(k, 1, 2)
            pl.when(inner)(lambda: line_event(k, 2, 3))
            arrived(k, z, 1 - y)
            when(outer, lambda: send(k, z, 1 - y, index(at(1), y, core), side_on_outer).start())
            odd = inner & (lax.rem(k, 2) == 1)
            when(odd, lambda: send(k, z, 1 - y, index(at(0), y, core), side_on_inner).start())

        def second_events(k):
            pl.when(outer)(lambda: line_event(k, 2, 3))
            arrived(k, at(beside), 1 - y)
            arrived(k, at(2), 1 - y)

        def third_events(k):
            arrived(k, at(3), 1 - y)
            give(k).start()
    else:
        offsets = range(1, layers)
        own_slots = [(lax.rem(z + s, layers), None, slot_of()) for s in offsets]
        own_across = slot_of()
        line_over = [slot_of() for _ in offsets]

        def direct_events(k):
            for place, s in enumerate(offsets):
                origin = lax.rem(z + s, layers)
                arrived(k, origin, y)
                send(k, origin, y, across, line_over[place]).start()

        def second_events(k):
            for s in range(layers):
                origin = lax.rem(z + s, layers)
                arrived(k, origin, 1 - y)

        def third_events(k):
            give(k).start()

    def own_events(k):
        send(k, z, y, across, own_across).start()
        for target, condition, number in own_slots:
            when(condition, lambda: send(k, z, y, index(target, y, core), number).start())

    def front(i, carry):
        slot = lax.rem(i, 2)
        weights = table[...]
        for c in range(local):
            if c % per_piece == 0:
                raw_load(i, c // per_piece).wait()
            trace = raw[slot, c]
            upper = trace.astype(jnp.bfloat16)
            lower = (trace - upper.astype(jnp.float32)).astype(jnp.bfloat16)
            spectra = jnp.dot(
                jnp.concatenate([upper, lower], axis=0), weights, preferred_element_type=jnp.float32
            )
            turned = (spectra[:block] + spectra[block:]).T
            value = turned[: 2 * band] + turned[2 * band :]
            for part in range(2):
                place = plan.order.index((part, c))
                for parity in range(2):
                    at_row = part * band + parity * pairs
                    rows[pl.ds(plan.row_of(parity, place), pairs, stride=plan.row_pitch), :] = value[
                        at_row : at_row + pairs
                    ]

        @pl.when(i + 2 < blocks)
        def _():
            raw_start(i + 2)

        for g in range(pairs):
            gathered[i, core, me // 2, g] = rows[g * plan.row_pitch : g * plan.row_pitch + plan.rows, :].astype(jnp.bfloat16)

        @pl.when(i == 0)
        def _():
            pl.semaphore_wait(barrier, n - 1)

        for g in range(groups):
            k = i * groups + g
            pl.when(k < AHEAD)(lambda: own_events(k))
        return carry

    lax.fori_loop(0, blocks, front, 0)

    for copy in side_loads:
        copy.wait()
    turn = 2.0 * math.pi / samples
    shift = move[...]
    weight = mask[...].astype(jnp.float32)
    phase = turn * lax.rem(FIRST_BIN * shift, samples).astype(jnp.float32)
    cosine[...] = weight * jnp.cos(phase)
    sine[...] = weight * jnp.sin(phase)
    phase = turn * shift.astype(jnp.float32)
    cos_step[...] = jnp.cos(phase)
    sin_step[...] = jnp.sin(phase)
    square[...] = jnp.zeros_like(square)
    energy[...] = jnp.zeros_like(energy)
    lined[...] = jnp.zeros_like(lined)
    mine[...] = jnp.zeros_like(mine)

    sub = lax.broadcasted_iota(jnp.int32, (8, templates), 0)

    def eight(origin, start, swap):
        wanted = plan.order[start : start + 8]
        result = None
        at_row = 0
        while at_row < 8:
            if at_row >= len(wanted):
                piece = jnp.zeros((8, templates), jnp.float32)
                end = 8
            else:
                part, c = wanted[at_row]
                end = at_row
                while end < len(wanted) and wanted[end] == (part, c + end - at_row):
                    end += 1
                source = 1 - part if swap else part
                piece = lined[pl.ds(8 + source * channels + origin * local + c - at_row, 8), :]
                if swap and part == 0:
                    piece = -piece
            result = piece if result is None else jnp.where(sub < at_row, result, piece)
            at_row = end
        return result

    def prepare(f, parity):
        c, s = cosine[...], sine[...]
        a = real[f].astype(jnp.float32)
        b = imag[f].astype(jnp.float32)
        whole_real = (a * c + b * s).astype(jnp.bfloat16).astype(jnp.float32)
        whole_imag = (b * c - a * s).astype(jnp.bfloat16).astype(jnp.float32)
        power = whole_real * whole_real + whole_imag * whole_imag
        square[...] += jnp.sum(power.reshape(channels // 8, 8, templates), axis=0)
        lined[pl.ds(8, channels), :] = whole_real
        lined[pl.ds(8 + channels, channels), :] = whole_imag
        c1, s1 = cos_step[...], sin_step[...]
        cosine[...] = c * c1 - s * s1
        sine[...] = s * c1 + c * s1
        blank = jnp.zeros((8, templates), jnp.float32)
        for swap in range(2):
            for tile in range(plan.tiles):
                parts = []
                for origin in [chip * 2 + side for side in range(2) for chip in range(n // 2)]:
                    if tile < plan.full or not plan.shared:
                        pair = [eight(origin, tile * TILE, swap == 1), eight(origin, tile * TILE + 8, swap == 1)]
                    else:
                        pair = [blank, blank]
                        pair[parity] = eight(origin, tile * TILE, swap == 1)
                    parts += pair
                turned = jnp.concatenate(parts, axis=0).astype(jnp.bfloat16).T
                eff[f, swap * templates : (swap + 1) * templates, tile * n * TILE : (tile + 1) * n * TILE] = turned

    def prepare_group(g):
        for copy in template_loads(g):
            copy.wait()

        def one(p, carry):
            for parity in range(2):
                prepare(2 * p + parity, parity)
            return carry

        lax.fori_loop(g * per_group, (g + 1) * per_group, one, 0)

    def cross_chunk(k):
        i, g = k // groups, lax.rem(k, groups)
        slot = lax.rem(i, 2)
        mates = shared_chunk(k, 1 - core)
        pltpu.make_async_copy(mates, mates, mate_sem.at[k]).wait()

        def one(p, carry):
            tiles = {}

            def load(row):
                if row not in tiles:
                    tiles[row] = gathered[i, :, :, p, row : row + TILE, :].reshape(n * TILE, block)
                return tiles[row]

            for parity in range(2):
                f = 2 * p + parity
                spec = jnp.concatenate([load(plan.tile_row(parity, tile)) for tile in range(plan.tiles)], axis=0)
                both = jnp.dot(eff[f], spec, preferred_element_type=jnp.float32)
                cross[slot, pl.ds(f, templates, stride=plan.pitch), :] = both[:templates]
                cross[slot, pl.ds(band + f, templates, stride=plan.pitch), :] = both[templates:]
            power = jnp.zeros((8, block), jnp.float32)
            for tile in tiles.values():
                value = tile.astype(jnp.float32)
                power += jnp.sum((value * value).reshape(n * TILE // 8, 8, block), axis=0)
            energy[i] += power
            return carry

        spread(g * per_group, per_group, CROSS_UNROLL, one, 0)

    scale = math.sqrt(2.0 * channels * band)
    octets = templates // 8 // groups

    def peak_part(q):
        i, part = q // groups, lax.rem(q, groups)
        slot = lax.rem(i, 2)
        inverse = inverse_ref[...]
        data_norm = jnp.sqrt(jnp.sum(energy[i], axis=0, keepdims=True) + epsilon)

        def octet(j, carry):
            bank = lax.rem(j, 4)
            for t in range(0, 8, 2):
                joined = jnp.concatenate(
                    [
                        cross[slot, pl.ds(pl.multiple_of((j * 8 + t + u) * plan.pitch, 8), 2 * band), :]
                        for u in range(2)
                    ],
                    axis=1,
                )
                upper = joined.astype(jnp.bfloat16)
                lower = (joined - upper.astype(jnp.float32)).astype(jnp.bfloat16)
                stacked = jnp.dot(
                    inverse, jnp.concatenate([upper, lower, upper], axis=0), preferred_element_type=jnp.float32
                )
                top = jnp.max(stacked.reshape(samples // 8, 8, 2 * block), axis=0)
                tops[bank, 8 * t : 8 * t + 8, :] = top[:, :block]
                tops[bank, 8 * t + 8 : 8 * t + 16, :] = top[:, block:]
            here = pl.ds(pl.multiple_of(j * 8, 8), 8)
            value = tops[bank, pl.ds(0, 8, stride=8), :]
            for s in range(1, 8):
                value = jnp.maximum(value, tops[bank, pl.ds(s, 8, stride=8), :])
            value = value * scale / (norm[here, :] * data_norm)
            peak_ref[here, pl.ds(pl.multiple_of(i * block, block), block)] = value
            return jnp.maximum(carry, value)

        lowest = jnp.full((8, block), -jnp.inf, jnp.float32)
        largest = spread(part * octets, octets, PEAK_UNROLL, octet, lowest)
        largest = jnp.max(largest, axis=0, keepdims=True)
        row = pl.ds(i, 1)
        mine[row, :] = jnp.where(part == 0, largest, jnp.maximum(mine[row, :], largest))

    def step(order, k, carry):
        def guarded(condition, action, index):
            pl.when(condition)(lambda: action(index))

        def finish_norm(k):
            total = jnp.sum(square[...], axis=0, keepdims=True)
            norm[...] = jnp.broadcast_to(jnp.sqrt(total + epsilon), (block, templates)).T

        peak_lag = CROSS + groups - 1
        work = {
            "cross": (k >= CROSS, cross_chunk, k - CROSS),
            "peak": (k >= peak_lag, peak_part, k - peak_lag),
            "own": (k + AHEAD < chunks, own_events, k + AHEAD),
            "direct": (k < chunks, direct_events, k),
            "second": ((k >= LAG) & (k < chunks + LAG), second_events, k - LAG),
            "third": ((k >= 2 * LAG) & (k < chunks + 2 * LAG), third_events, k - 2 * LAG),
            "prepare": (k < groups, prepare_group, k),
            "norm": (k == groups, finish_norm, k),
        }
        for name in order:
            guarded(*work[name])
        return carry

    lax.fori_loop(0, chunks, functools.partial(step, ORDER), 0)
    lax.fori_loop(chunks, chunks + CROSS, functools.partial(step, LATE), 0)

    def last(q, carry):
        peak_part(q)
        return carry

    lax.fori_loop(chunks + 1 - groups, chunks, last, 0)

    def best_copy(step):
        return pltpu.make_async_remote_copy(
            src_ref=mine, dst_ref=slots.at[step - 1], send_sem=best_send.at[0], recv_sem=best_recv.at[0],
            device_id={"row": lax.rem(me + step, n)}, device_id_type=MESH,
        )

    def best_start(step, carry):
        best_copy(step).start()
        return carry

    lax.fori_loop(1, n, best_start, 0)
    for number, (condition, share) in enumerate(sent):
        ref = gathered.at[:, 0, 0] if share == 1 else gathered.at[:, 0, 0, pl.ds(0, pairs // share)]
        wait = pltpu.make_async_remote_copy(
            src_ref=ref, dst_ref=ref, send_sem=send_sem.at[number], recv_sem=recv_sem.at[0, 0],
            device_id={"row": partner}, device_id_type=MESH,
        )
        when(condition, wait.wait_send)
    whole = gathered.at[:, 0]
    pltpu.make_async_remote_copy(
        src_ref=whole, dst_ref=whole, send_sem=give_sem.at[0], recv_sem=recv_sem.at[0, 0],
        device_id={"row": partner}, device_id_type=MESH,
    ).wait_send()
    everyone = slots.at[pl.ds(0, n - 1)]
    all_best = pltpu.make_async_remote_copy(
        src_ref=everyone, dst_ref=everyone, send_sem=best_send.at[0], recv_sem=best_recv.at[0],
        device_id={"row": partner}, device_id_type=MESH,
    )
    all_best.wait()
    best_ref[...] = jnp.maximum(mine[...], jnp.max(slots[...], axis=0))


def finish_kernel(blocks, peak_ref, best_ref, peak_out, best_out):
    block = best_ref.shape[1]
    for i in range(blocks):
        best_out[pl.ds(i * block, block)] = best_ref[i]
    peak_out[...] = peak_ref[...]


def send_slots(plan):
    if plan.layers == 4 and plan.groups % 2 == 0:
        return 10
    return 2 * plan.layers - 1


def body(n, raw_trace, fir_taps, templ_real, templ_imag, channel_mask, moveout):
    local, windows, length = raw_trace.shape
    samples = length // 2
    band, channels, templates = templ_real.shape
    plan = Plan(n, local, band, samples, templates, windows)
    bins = FIRST_BIN + np.arange(band)
    lags = np.arange(samples)
    angle = 2.0 * np.pi / samples * (bins[:, None] * lags[None, :] % samples)
    inverse = np.concatenate([np.cos(angle), -np.sin(angle)], axis=0)

    span = (fir_taps.shape[0] + 1) // 2
    forward = np.zeros((samples + span + 1, 2 * band))
    forward[:samples] = np.concatenate([inverse[:band][::2], inverse[:band][1::2], inverse[band:][::2], inverse[band:][1::2]]).T
    padded = -(-(samples + span) // 8) * 8
    both = np.zeros((padded, 4 * band), np.float32)
    both[: samples + span, : 2 * band] = forward[:-1]
    both[: samples + span, 2 * band :] = forward[1:]
    forward = jnp.asarray(both)

    inverse = inverse.T.astype(np.float32)
    high = inverse.astype(jnp.bfloat16)
    low = (inverse - high.astype(np.float32)).astype(jnp.bfloat16)
    inverse3 = jnp.asarray(np.concatenate([high, high, low], axis=1))

    vmem = pl.BlockSpec(memory_space=pltpu.VMEM)
    anywhere = pl.BlockSpec(memory_space=pl.ANY)
    f32, bf16 = jnp.float32, jnp.bfloat16
    pieces = math.gcd(local, 4)
    best_rows = -(-plan.blocks // 8) * 8
    peak, best = pl.pallas_call(
        functools.partial(scan_kernel, plan),
        out_shape=(
            jax.ShapeDtypeStruct((templates, windows), f32),
            jax.ShapeDtypeStruct((best_rows, plan.block), f32),
        ),
        in_specs=[pl.BlockSpec(memory_space=pltpu.SMEM), vmem, vmem] + [anywhere] * 5,
        out_specs=(vmem, vmem),
        scratch_shapes=[
            pltpu.VMEM((plan.blocks, 2, n // 2, plan.pairs, plan.rows, plan.block), bf16),
            pltpu.VMEM((band, 2 * templates, plan.depth), bf16),
            pltpu.VMEM((2, templates * plan.pitch, plan.block), f32),
            pltpu.VMEM((2, local, plan.block, length), f32),
            pltpu.VMEM((length, 4 * band), bf16),
            pltpu.VMEM((length, 4 * band), f32),
            pltpu.VMEM((plan.pairs * plan.row_pitch, plan.block), f32),
            pltpu.VMEM((band, channels, templates), bf16),
            pltpu.VMEM((band, channels, templates), bf16),
            pltpu.VMEM((channels, templates), jnp.int32),
            pltpu.VMEM((channels, templates), jnp.int32),
            pltpu.VMEM((channels, templates), f32),
            pltpu.VMEM((channels, templates), f32),
            pltpu.VMEM((channels, templates), f32),
            pltpu.VMEM((channels, templates), f32),
            pltpu.VMEM((2 * channels + 16, templates), f32),
            pltpu.VMEM((8, templates), f32),
            pltpu.VMEM((plan.blocks, 8, plan.block), f32),
            pltpu.VMEM((templates, plan.block), f32),
            pltpu.VMEM((4, 64, plan.block), f32),
            pltpu.VMEM((best_rows, plan.block), f32),
            pltpu.VMEM((n - 1, best_rows, plan.block), f32),
            pltpu.SemaphoreType.DMA((2, pieces)),
            pltpu.SemaphoreType.DMA((2,)),
            pltpu.SemaphoreType.DMA((2, plan.groups)),
            pltpu.SemaphoreType.DMA((plan.chunks, n // 2)),
            pltpu.SemaphoreType.DMA((plan.chunks,)),
            pltpu.SemaphoreType.DMA((1,)),
            pltpu.SemaphoreType.DMA((send_slots(plan),)),
            pltpu.SemaphoreType.DMA((1,)),
            pltpu.SemaphoreType.DMA((1,)),
        ],
        compiler_params=pltpu.CompilerParams(
            collective_id=0, has_side_effects=True, vmem_limit_bytes=VMEM_LIMIT
        ),
        name="gather_scan",
    )(fir_taps, forward, inverse3, channel_mask, moveout, raw_trace, templ_real, templ_imag)
    peak, best = pl.pallas_call(
        functools.partial(finish_kernel, plan.blocks),
        out_shape=(jax.ShapeDtypeStruct((templates, windows), f32), jax.ShapeDtypeStruct((windows,), f32)),
        in_specs=[vmem, vmem],
        out_specs=(vmem, vmem),

        name="finish",
    )(peak, best)
    return (peak, best)


def solution(mesh):
    in_specs = (
        P("row", "parts", None),
        P(),
        P(None, None, "row"),
        P(None, None, "row"),
        P(None, "row"),
        P(None, "row"),
    )
    out_specs = (P("row", "parts"), P("parts"))
    return jax.shard_map(
        functools.partial(body, mesh.shape["row"]),
        mesh=mesh,
        in_specs=in_specs,
        out_specs=out_specs,
        check_vma=False,
    )
```

```python
import functools
import math

import jax
import jax.numpy as jnp
import numpy as np
from jax import lax
from jax.experimental import pallas as pl
from jax.experimental.pallas import tpu as pltpu
from jax.sharding import PartitionSpec as P

FIRST_BIN = 16
TILE = 16
AHEAD = 3
CROSS_UNROLL = 4
PEAK_UNROLL = 4
LAST_UNROLL = 8
LAG = 2
CROSS = 2 * LAG + 1
ORDER = ("norm", "own", "direct", "second", "third", "cross", "peak", "prepare")
LATE = ("second", "third", "cross", "catch_up")

epsilon = 1e-06
VMEM_LIMIT = 62 * 1024 * 1024
MESH = pl.DeviceIdType.MESH


class Plan:
    def __init__(self, n, local, band, samples, templates, windows):
        self.n, self.local, self.band, self.samples = n, local, band, samples
        self.templates, self.windows = templates, windows
        self.block = math.gcd(windows, 128)
        self.blocks = windows // self.block
        self.pairs = band // 2
        self.groups = math.gcd(self.pairs, 4)
        self.per_group = self.pairs // self.groups
        self.chunks = self.blocks * self.groups
        self.layers = n // 4
        whole = local - local % 8
        self.order = (
            [(0, c) for c in range(whole)]
            + [(1, c) for c in range(whole)]
            + [(part, c) for part in range(2) for c in range(whole, local)]
        )
        count = len(self.order)
        self.full = count // TILE
        self.rest = count - self.full * TILE
        self.shared = 0 < self.rest <= 8
        self.tiles = self.full + (1 if self.rest else 0)
        self.rows = 2 * TILE * self.full + (0 if not self.rest else TILE if self.shared else 2 * TILE)
        self.depth = self.tiles * n * TILE
        self.pitch = 2 * band + 8
        self.row_pitch = self.rows + 8

    def row_of(self, parity, place):
        base = TILE * self.full
        if place < base:
            return parity * base + place
        if self.shared:
            return 2 * base + 8 * parity + place - base
        return 2 * base + TILE * parity + place - base

    def tile_row(self, parity, tile):
        if tile < self.full:
            return parity * TILE * self.full + tile * TILE
        return 2 * TILE * self.full + (0 if self.shared else TILE * parity)


def scan_kernel(
    plan, taps_ref, forward_ref, inverse_ref, mask_ref, move_ref, raw_ref, real_ref, imag_ref, peak_ref, best_ref,
    gathered, eff, cross, raw, table, wide, rows, real, imag, mask, move, cosine, sine, cos_step, sin_step, lined,
    square, energy, norm, tops, mine, slots,
    raw_sem, side_sem, load_sem, recv_sem, mate_sem, give_sem, send_sem, best_send, best_recv,
):
    n, layers, block, blocks = plan.n, plan.layers, plan.block, plan.blocks
    groups, per_group, chunks, pairs = plan.groups, plan.per_group, plan.chunks, plan.pairs
    band, templates, local, samples = plan.band, plan.templates, plan.local, plan.samples
    channels = n * local
    length = 2 * samples
    taps = taps_ref.shape[0]
    me = lax.axis_index("row")
    z, y, core = me // 4, lax.rem(me // 2, 2), lax.rem(me, 2)

    def index(z, y, core):
        return z * 4 + y * 2 + core

    partner = index(z, y, 1 - core)
    across = index(z, 1 - y, core)

    def spread(begin, count, unroll, action, value):
        unroll = math.gcd(count, unroll)

        def several(j, carry):
            for u in range(unroll):
                carry = action(begin + j * unroll + u, carry)
            return carry

        return several(0, value) if unroll == count else lax.fori_loop(0, count // unroll, several, value)

    barrier = pltpu.get_barrier_semaphore()

    def greet(step, carry):
        pl.semaphore_signal(barrier, inc=1, device_id={"row": lax.rem(me + step, n)}, device_id_type=MESH)
        return carry

    lax.fori_loop(1, n, greet, 0)

    pieces = math.gcd(local, 4)
    per_piece = local // pieces

    def raw_load(i, p):
        slot = lax.rem(i, 2)
        return pltpu.make_async_copy(
            raw_ref.at[pl.ds(p * per_piece, per_piece), pl.ds(pl.multiple_of(i * block, block), block)],
            raw.at[slot, pl.ds(p * per_piece, per_piece)],
            raw_sem.at[slot, p],
        )

    def raw_start(i):
        for p in range(pieces):
            raw_load(i, p).start()

    def template_loads(g):
        bins = pl.ds(g * 2 * per_group, 2 * per_group)
        return [
            pltpu.make_async_copy(real_ref.at[bins], real.at[bins], load_sem.at[0, g]),
            pltpu.make_async_copy(imag_ref.at[bins], imag.at[bins], load_sem.at[1, g]),
        ]

    side_loads = [
        pltpu.make_async_copy(mask_ref, mask, side_sem.at[0]),
        pltpu.make_async_copy(move_ref, move, side_sem.at[1]),
    ]
    raw_start(0)
    if blocks > 1:
        raw_start(1)
    for copy in side_loads:
        copy.start()
    for g in range(groups):
        for copy in template_loads(g):
            copy.start()

    lane = lax.broadcasted_iota(jnp.int32, (8, 128), 1)
    low_half = lane < 2 * band
    total = jnp.zeros((samples, 128), jnp.float32)
    for i in range((taps + 1) // 2):
        odd = taps_ref[2 * i + 1] if 2 * i + 1 < taps else 0.0
        factor = jnp.where(low_half, taps_ref[2 * i], odd)[:1]
        total = total + factor * forward_ref[pl.ds(i, samples), :]
    high = total.astype(jnp.bfloat16).astype(jnp.float32)
    low = total - high
    half = low_half[:1]
    wide[pl.ds(0, samples, stride=2), :] = jnp.where(half, high, pltpu.roll(low, 2 * band, 1))
    wide[pl.ds(1, samples, stride=2), :] = jnp.where(half, pltpu.roll(high, 2 * band, 1), low)
    table[...] = wide[...].astype(jnp.bfloat16)
    if plan.rows * pairs != 2 * local * band:
        rows[...] = jnp.zeros_like(rows)

    def chunk(k, zo, yo):
        i, g = k // groups, lax.rem(k, groups)
        return gathered.at[i, core, zo * 2 + yo, pl.ds(g * per_group, per_group)]

    def shared_chunk(k, side):
        i, g = k // groups, lax.rem(k, groups)
        return gathered.at[i, side, :, pl.ds(g * per_group, per_group)]

    def send(k, zo, yo, target, slot):
        ref = chunk(k, zo, yo)
        return pltpu.make_async_remote_copy(
            src_ref=ref, dst_ref=ref, send_sem=send_sem.at[slot], recv_sem=recv_sem.at[k, zo * 2 + yo],
            device_id={"row": target}, device_id_type=MESH,
        )

    def give(k):
        ref = shared_chunk(k, core)
        return pltpu.make_async_remote_copy(
            src_ref=ref, dst_ref=ref, send_sem=give_sem.at[0], recv_sem=mate_sem.at[k],
            device_id={"row": partner}, device_id_type=MESH,
        )

    def arrived(k, zo, yo):
        send(k, zo, yo, partner, 0).wait_recv()

    near = layers == 4 and groups % 2 == 0
    sent = []

    def slot_of(condition=None, share=1):
        sent.append((condition, share))
        return len(sent) - 1

    def when(condition, action):
        if condition is None:
            action()
        else:
            pl.when(condition)(action)

    if near:
        far = z >= 2
        depth_of = jnp.where(far, 3 - z, z)
        inner, outer = depth_of == 1, depth_of == 0

        def at(q):
            return jnp.where(far, 3 - q, q)

        beside = 1 - depth_of
        own_slots = [(at(beside), None, slot_of()), (at(2), None, slot_of()), (at(3), inner, slot_of(inner))]
        own_across = slot_of()
        line_over = [slot_of(outer, 2), slot_of(), slot_of()]
        line_on = slot_of(inner)
        side_on_outer, side_on_inner = slot_of(outer), slot_of(inner, 2)

        def line_event(k, place, q):
            origin = at(q)
            arrived(k, origin, y)
            condition = outer & (lax.rem(k, 2) == 0) if place == 0 else None
            when(condition, lambda: send(k, origin, y, across, line_over[place]).start())
            if place == 2:
                when(inner, lambda: send(k, origin, y, index(at(0), y, core), line_on).start())

        def direct_events(k):
            line_event(k, 0, beside)
            line_event(k, 1, 2)
            pl.when(inner)(lambda: line_event(k, 2, 3))
            arrived(k, z, 1 - y)
            when(outer, lambda: send(k, z, 1 - y, index(at(1), y, core), side_on_outer).start())
            odd = inner & (lax.rem(k, 2) == 1)
            when(odd, lambda: send(k, z, 1 - y, index(at(0), y, core), side_on_inner).start())

        def second_events(k):
            pl.when(outer)(lambda: line_event(k, 2, 3))
            arrived(k, at(beside), 1 - y)
            arrived(k, at(2), 1 - y)

        def third_events(k):
            arrived(k, at(3), 1 - y)
            give(k).start()
    else:
        offsets = range(1, layers)
        own_slots = [(lax.rem(z + s, layers), None, slot_of()) for s in offsets]
        own_across = slot_of()
        line_over = [slot_of() for _ in offsets]

        def direct_events(k):
            for place, s in enumerate(offsets):
                origin = lax.rem(z + s, layers)
                arrived(k, origin, y)
                send(k, origin, y, across, line_over[place]).start()

        def second_events(k):
            for s in range(layers):
                origin = lax.rem(z + s, layers)
                arrived(k, origin, 1 - y)

        def third_events(k):
            give(k).start()

    def own_events(k):
        send(k, z, y, across, own_across).start()
        for target, condition, number in own_slots:
            when(condition, lambda: send(k, z, y, index(target, y, core), number).start())

    def front(i, carry):
        slot = lax.rem(i, 2)
        weights = table[...]
        for c in range(local):
            if c % per_piece == 0:
                raw_load(i, c // per_piece).wait()
            trace = raw[slot, c]
            upper = trace.astype(jnp.bfloat16)
            lower = (trace - upper.astype(jnp.float32)).astype(jnp.bfloat16)
            spectra = jnp.dot(
                jnp.concatenate([upper, lower], axis=0), weights, preferred_element_type=jnp.float32
            )
            turned = (spectra[:block] + spectra[block:]).T
            value = turned[: 2 * band] + turned[2 * band :]
            for part in range(2):
                place = plan.order.index((part, c))
                for parity in range(2):
                    at_row = part * band + parity * pairs
                    rows[pl.ds(plan.row_of(parity, place), pairs, stride=plan.row_pitch), :] = value[
                        at_row : at_row + pairs
                    ]

        @pl.when(i + 2 < blocks)
        def _():
            raw_start(i + 2)

        for g in range(pairs):
            gathered[i, core, me // 2, g] = rows[g * plan.row_pitch : g * plan.row_pitch + plan.rows, :].astype(jnp.bfloat16)

        @pl.when(i == 0)
        def _():
            pl.semaphore_wait(barrier, n - 1)

        for g in range(groups):
            k = i * groups + g
            pl.when(k < AHEAD)(lambda: own_events(k))
        return carry

    lax.fori_loop(0, blocks, front, 0)

    for copy in side_loads:
        copy.wait()
    turn = 2.0 * math.pi / samples
    shift = move[...]
    weight = mask[...].astype(jnp.float32)
    phase = turn * lax.rem(FIRST_BIN * shift, samples).astype(jnp.float32)
    cosine[...] = weight * jnp.cos(phase)
    sine[...] = weight * jnp.sin(phase)
    phase = turn * shift.astype(jnp.float32)
    cos_step[...] = jnp.cos(phase)
    sin_step[...] = jnp.sin(phase)
    square[...] = jnp.zeros_like(square)
    energy[...] = jnp.zeros_like(energy)
    lined[...] = jnp.zeros_like(lined)
    mine[...] = jnp.zeros_like(mine)

    sub = lax.broadcasted_iota(jnp.int32, (8, templates), 0)

    def eight(origin, start, swap):
        wanted = plan.order[start : start + 8]
        result = None
        at_row = 0
        while at_row < 8:
            if at_row >= len(wanted):
                piece = jnp.zeros((8, templates), jnp.float32)
                end = 8
            else:
                part, c = wanted[at_row]
                end = at_row
                while end < len(wanted) and wanted[end] == (part, c + end - at_row):
                    end += 1
                source = 1 - part if swap else part
                piece = lined[pl.ds(8 + source * channels + origin * local + c - at_row, 8), :]
                if swap and part == 0:
                    piece = -piece
            result = piece if result is None else jnp.where(sub < at_row, result, piece)
            at_row = end
        return result

    def prepare(f, parity):
        c, s = cosine[...], sine[...]
        a = real[f].astype(jnp.float32)
        b = imag[f].astype(jnp.float32)
        whole_real = (a * c + b * s).astype(jnp.bfloat16).astype(jnp.float32)
        whole_imag = (b * c - a * s).astype(jnp.bfloat16).astype(jnp.float32)
        power = whole_real * whole_real + whole_imag * whole_imag
        square[...] += jnp.sum(power.reshape(channels // 8, 8, templates), axis=0)
        lined[pl.ds(8, channels), :] = whole_real
        lined[pl.ds(8 + channels, channels), :] = whole_imag
        c1, s1 = cos_step[...], sin_step[...]
        cosine[...] = c * c1 - s * s1
        sine[...] = s * c1 + c * s1
        blank = jnp.zeros((8, templates), jnp.float32)
        for swap in range(2):
            for tile in range(plan.tiles):
                parts = []
                for origin in [chip * 2 + side for side in range(2) for chip in range(n // 2)]:
                    if tile < plan.full or not plan.shared:
                        pair = [eight(origin, tile * TILE, swap == 1), eight(origin, tile * TILE + 8, swap == 1)]
                    else:
                        pair = [blank, blank]
                        pair[parity] = eight(origin, tile * TILE, swap == 1)
                    parts += pair
                turned = jnp.concatenate(parts, axis=0).astype(jnp.bfloat16).T
                eff[f, swap * templates : (swap + 1) * templates, tile * n * TILE : (tile + 1) * n * TILE] = turned

    def prepare_group(g):
        for copy in template_loads(g):
            copy.wait()

        def one(p, carry):
            for parity in range(2):
                prepare(2 * p + parity, parity)
            return carry

        lax.fori_loop(g * per_group, (g + 1) * per_group, one, 0)

    def cross_chunk(k):
        i, g = k // groups, lax.rem(k, groups)
        slot = lax.rem(i, 2)
        mates = shared_chunk(k, 1 - core)
        pltpu.make_async_copy(mates, mates, mate_sem.at[k]).wait()

        def one(p, carry):
            tiles = {}

            def load(row):
                if row not in tiles:
                    tiles[row] = gathered[i, :, :, p, row : row + TILE, :].reshape(n * TILE, block)
                return tiles[row]

            for parity in range(2):
                f = 2 * p + parity
                spec = jnp.concatenate([load(plan.tile_row(parity, tile)) for tile in range(plan.tiles)], axis=0)
                both = jnp.dot(eff[f], spec, preferred_element_type=jnp.float32)
                cross[slot, pl.ds(f, templates, stride=plan.pitch), :] = both[:templates]
                cross[slot, pl.ds(band + f, templates, stride=plan.pitch), :] = both[templates:]
            power = jnp.zeros((8, block), jnp.float32)
            for tile in tiles.values():
                value = tile.astype(jnp.float32)
                power += jnp.sum((value * value).reshape(n * TILE // 8, 8, block), axis=0)
            energy[i] += power
            return carry

        spread(g * per_group, per_group, CROSS_UNROLL, one, 0)

    scale = math.sqrt(2.0 * channels * band)
    octets = templates // 8 // groups

    def peak_part(q):
        i, part = q // groups, lax.rem(q, groups)
        peak_range(i, part * octets, octets, PEAK_UNROLL, part == 0)

    def peak_range(i, begin, count, unroll, fresh):
        slot = lax.rem(i, 2)
        inverse = inverse_ref[...]
        data_norm = jnp.sqrt(jnp.sum(energy[i], axis=0, keepdims=True) + epsilon)

        def octet(j, carry):
            bank = lax.rem(j, 4)
            for t in range(0, 8, 2):
                joined = jnp.concatenate(
                    [
                        cross[slot, pl.ds(pl.multiple_of((j * 8 + t + u) * plan.pitch, 8), 2 * band), :]
                        for u in range(2)
                    ],
                    axis=1,
                )
                upper = joined.astype(jnp.bfloat16)
                lower = (joined - upper.astype(jnp.float32)).astype(jnp.bfloat16)
                stacked = jnp.dot(
                    inverse, jnp.concatenate([upper, lower, upper], axis=0), preferred_element_type=jnp.float32
                )
                top = jnp.max(stacked.reshape(samples // 8, 8, 2 * block), axis=0)
                tops[bank, 8 * t : 8 * t + 8, :] = top[:, :block]
                tops[bank, 8 * t + 8 : 8 * t + 16, :] = top[:, block:]
            here = pl.ds(pl.multiple_of(j * 8, 8), 8)
            value = tops[bank, pl.ds(0, 8, stride=8), :]
            for s in range(1, 8):
                value = jnp.maximum(value, tops[bank, pl.ds(s, 8, stride=8), :])
            value = value * scale / (norm[here, :] * data_norm)
            peak_ref[here, pl.ds(pl.multiple_of(i * block, block), block)] = value
            return jnp.maximum(carry, value)

        lowest = jnp.full((8, block), -jnp.inf, jnp.float32)
        largest = spread(begin, count, unroll, octet, lowest)
        largest = jnp.max(largest, axis=0, keepdims=True)
        row = pl.ds(i, 1)
        mine[row, :] = jnp.where(fresh, largest, jnp.maximum(mine[row, :], largest))

    peak_lag = CROSS + groups - 1

    def step(order, k, carry):
        def guarded(condition, action, index):
            pl.when(condition)(lambda: action(index))

        def finish_norm(k):
            total = jnp.sum(square[...], axis=0, keepdims=True)
            norm[...] = jnp.broadcast_to(jnp.sqrt(total + epsilon), (block, templates)).T

        def catch_up(k):
            for u in range(2):
                peak_part(2 * k - chunks - peak_lag + u)

        work = {
            "cross": (k >= CROSS, cross_chunk, k - CROSS),
            "peak": (k >= peak_lag, peak_part, k - peak_lag),
            "own": (k + AHEAD < chunks, own_events, k + AHEAD),
            "direct": (k < chunks, direct_events, k),
            "second": ((k >= LAG) & (k < chunks + LAG), second_events, k - LAG),
            "third": ((k >= 2 * LAG) & (k < chunks + 2 * LAG), third_events, k - 2 * LAG),
            "prepare": (k < groups, prepare_group, k),
            "catch_up": ((k < chunks + LAG) & (2 * k >= chunks + peak_lag), catch_up, k),
            "norm": (k == groups, finish_norm, k),
        }
        for name in order:
            guarded(*work[name])
        return carry

    lax.fori_loop(0, chunks, functools.partial(step, ORDER), 0)
    lax.fori_loop(chunks, chunks + CROSS, functools.partial(step, LATE), 0)

    peak_range(blocks - 1, 0, templates // 8, LAST_UNROLL, True)

    def best_copy(step):
        return pltpu.make_async_remote_copy(
            src_ref=mine, dst_ref=slots.at[step - 1], send_sem=best_send.at[0], recv_sem=best_recv.at[0],
            device_id={"row": lax.rem(me + step, n)}, device_id_type=MESH,
        )

    def best_start(step, carry):
        best_copy(step).start()
        return carry

    lax.fori_loop(1, n, best_start, 0)
    for number, (condition, share) in enumerate(sent):
        ref = gathered.at[:, 0, 0] if share == 1 else gathered.at[:, 0, 0, pl.ds(0, pairs // share)]
        wait = pltpu.make_async_remote_copy(
            src_ref=ref, dst_ref=ref, send_sem=send_sem.at[number], recv_sem=recv_sem.at[0, 0],
            device_id={"row": partner}, device_id_type=MESH,
        )
        when(condition, wait.wait_send)
    whole = gathered.at[:, 0]
    pltpu.make_async_remote_copy(
        src_ref=whole, dst_ref=whole, send_sem=give_sem.at[0], recv_sem=recv_sem.at[0, 0],
        device_id={"row": partner}, device_id_type=MESH,
    ).wait_send()
    everyone = slots.at[pl.ds(0, n - 1)]
    all_best = pltpu.make_async_remote_copy(
        src_ref=everyone, dst_ref=everyone, send_sem=best_send.at[0], recv_sem=best_recv.at[0],
        device_id={"row": partner}, device_id_type=MESH,
    )
    all_best.wait()
    best_ref[...] = jnp.maximum(mine[...], jnp.max(slots[...], axis=0))


def finish_kernel(blocks, peak_ref, best_ref, peak_out, best_out):
    block = best_ref.shape[1]
    for i in range(blocks):
        best_out[pl.ds(i * block, block)] = best_ref[i]
    peak_out[...] = peak_ref[...]


def send_slots(plan):
    if plan.layers == 4 and plan.groups % 2 == 0:
        return 10
    return 2 * plan.layers - 1


def body(n, raw_trace, fir_taps, templ_real, templ_imag, channel_mask, moveout):
    local, windows, length = raw_trace.shape
    samples = length // 2
    band, channels, templates = templ_real.shape
    plan = Plan(n, local, band, samples, templates, windows)
    bins = FIRST_BIN + np.arange(band)
    lags = np.arange(samples)
    angle = 2.0 * np.pi / samples * (bins[:, None] * lags[None, :] % samples)
    inverse = np.concatenate([np.cos(angle), -np.sin(angle)], axis=0)

    span = (fir_taps.shape[0] + 1) // 2
    forward = np.zeros((samples + span + 1, 2 * band))
    forward[:samples] = np.concatenate([inverse[:band][::2], inverse[:band][1::2], inverse[band:][::2], inverse[band:][1::2]]).T
    padded = -(-(samples + span) // 8) * 8
    both = np.zeros((padded, 4 * band), np.float32)
    both[: samples + span, : 2 * band] = forward[:-1]
    both[: samples + span, 2 * band :] = forward[1:]
    forward = jnp.asarray(both)

    inverse = inverse.T.astype(np.float32)
    high = inverse.astype(jnp.bfloat16)
    low = (inverse - high.astype(np.float32)).astype(jnp.bfloat16)
    inverse3 = jnp.asarray(np.concatenate([high, high, low], axis=1))

    vmem = pl.BlockSpec(memory_space=pltpu.VMEM)
    anywhere = pl.BlockSpec(memory_space=pl.ANY)
    f32, bf16 = jnp.float32, jnp.bfloat16
    pieces = math.gcd(local, 4)
    best_rows = -(-plan.blocks // 8) * 8
    peak, best = pl.pallas_call(
        functools.partial(scan_kernel, plan),
        out_shape=(
            jax.ShapeDtypeStruct((templates, windows), f32),
            jax.ShapeDtypeStruct((best_rows, plan.block), f32),
        ),
        in_specs=[pl.BlockSpec(memory_space=pltpu.SMEM), vmem, vmem] + [anywhere] * 5,
        out_specs=(vmem, vmem),
        scratch_shapes=[
            pltpu.VMEM((plan.blocks, 2, n // 2, plan.pairs, plan.rows, plan.block), bf16),
            pltpu.VMEM((band, 2 * templates, plan.depth), bf16),
            pltpu.VMEM((2, templates * plan.pitch, plan.block), f32),
            pltpu.VMEM((2, local, plan.block, length), f32),
            pltpu.VMEM((length, 4 * band), bf16),
            pltpu.VMEM((length, 4 * band), f32),
            pltpu.VMEM((plan.pairs * plan.row_pitch, plan.block), f32),
            pltpu.VMEM((band, channels, templates), bf16),
            pltpu.VMEM((band, channels, templates), bf16),
            pltpu.VMEM((channels, templates), jnp.int32),
            pltpu.VMEM((channels, templates), jnp.int32),
            pltpu.VMEM((channels, templates), f32),
            pltpu.VMEM((channels, templates), f32),
            pltpu.VMEM((channels, templates), f32),
            pltpu.VMEM((channels, templates), f32),
            pltpu.VMEM((2 * channels + 16, templates), f32),
            pltpu.VMEM((8, templates), f32),
            pltpu.VMEM((plan.blocks, 8, plan.block), f32),
            pltpu.VMEM((templates, plan.block), f32),
            pltpu.VMEM((4, 64, plan.block), f32),
            pltpu.VMEM((best_rows, plan.block), f32),
            pltpu.VMEM((n - 1, best_rows, plan.block), f32),
            pltpu.SemaphoreType.DMA((2, pieces)),
            pltpu.SemaphoreType.DMA((2,)),
            pltpu.SemaphoreType.DMA((2, plan.groups)),
            pltpu.SemaphoreType.DMA((plan.chunks, n // 2)),
            pltpu.SemaphoreType.DMA((plan.chunks,)),
            pltpu.SemaphoreType.DMA((1,)),
            pltpu.SemaphoreType.DMA((send_slots(plan),)),
            pltpu.SemaphoreType.DMA((1,)),
            pltpu.SemaphoreType.DMA((1,)),
        ],
        compiler_params=pltpu.CompilerParams(
            collective_id=0, has_side_effects=True, vmem_limit_bytes=VMEM_LIMIT
        ),
        name="gather_scan",
    )(fir_taps, forward, inverse3, channel_mask, moveout, raw_trace, templ_real, templ_imag)
    peak, best = pl.pallas_call(
        functools.partial(finish_kernel, plan.blocks),
        out_shape=(jax.ShapeDtypeStruct((templates, windows), f32), jax.ShapeDtypeStruct((windows,), f32)),
        in_specs=[vmem, vmem],
        out_specs=(vmem, vmem),

        name="finish",
    )(peak, best)
    return (peak, best)


def solution(mesh):
    in_specs = (
        P("row", "parts", None),
        P(),
        P(None, None, "row"),
        P(None, None, "row"),
        P(None, "row"),
        P(None, "row"),
    )
    out_specs = (P("row", "parts"), P("parts"))
    return jax.shard_map(
        functools.partial(body, mesh.shape["row"]),
        mesh=mesh,
        in_specs=in_specs,
        out_specs=out_specs,
        check_vma=False,
    )
```

```python
import functools
import math

import jax
import jax.numpy as jnp
import numpy as np
from jax import lax
from jax.experimental import pallas as pl
from jax.experimental.pallas import tpu as pltpu
from jax.sharding import PartitionSpec as P

FIRST_BIN = 16
TILE = 16
AHEAD = 3
CROSS_UNROLL = 4
PEAK_UNROLL = 4
LAST_UNROLL = 16
LAG = 2
CROSS = 2 * LAG + 1
ORDER = ("norm", "own", "direct", "second", "third", "cross", "peak", "prepare")
LATE = ("second", "third", "cross", "catch_up")

epsilon = 1e-06
VMEM_LIMIT = 62 * 1024 * 1024
MESH = pl.DeviceIdType.MESH


class Plan:
    def __init__(self, n, local, band, samples, templates, windows):
        self.n, self.local, self.band, self.samples = n, local, band, samples
        self.templates, self.windows = templates, windows
        self.block = math.gcd(windows, 128)
        self.blocks = windows // self.block
        self.pairs = band // 2
        self.groups = math.gcd(self.pairs, 4)
        self.per_group = self.pairs // self.groups
        self.chunks = self.blocks * self.groups
        self.layers = n // 4
        whole = local - local % 8
        self.order = (
            [(0, c) for c in range(whole)]
            + [(1, c) for c in range(whole)]
            + [(part, c) for part in range(2) for c in range(whole, local)]
        )
        count = len(self.order)
        self.full = count // TILE
        self.rest = count - self.full * TILE
        self.shared = 0 < self.rest <= 8
        self.tiles = self.full + (1 if self.rest else 0)
        self.rows = 2 * TILE * self.full + (0 if not self.rest else TILE if self.shared else 2 * TILE)
        self.depth = self.tiles * n * TILE
        self.pitch = 2 * band + 8
        self.row_pitch = self.rows + 8

    def row_of(self, parity, place):
        base = TILE * self.full
        if place < base:
            return parity * base + place
        if self.shared:
            return 2 * base + 8 * parity + place - base
        return 2 * base + TILE * parity + place - base

    def tile_row(self, parity, tile):
        if tile < self.full:
            return parity * TILE * self.full + tile * TILE
        return 2 * TILE * self.full + (0 if self.shared else TILE * parity)


def scan_kernel(
    plan, taps_ref, forward_ref, inverse_ref, mask_ref, move_ref, raw_ref, real_ref, imag_ref, peak_ref, best_ref,
    gathered, eff, cross, raw, table, wide, rows, real, imag, mask, move, cosine, sine, cos_step, sin_step, lined,
    square, energy, norm, tops, mine, slots,
    raw_sem, side_sem, load_sem, recv_sem, mate_sem, give_sem, send_sem, best_send, best_recv,
):
    n, layers, block, blocks = plan.n, plan.layers, plan.block, plan.blocks
    groups, per_group, chunks, pairs = plan.groups, plan.per_group, plan.chunks, plan.pairs
    band, templates, local, samples = plan.band, plan.templates, plan.local, plan.samples
    channels = n * local
    length = 2 * samples
    taps = taps_ref.shape[0]
    me = lax.axis_index("row")
    z, y, core = me // 4, lax.rem(me // 2, 2), lax.rem(me, 2)

    def index(z, y, core):
        return z * 4 + y * 2 + core

    partner = index(z, y, 1 - core)
    across = index(z, 1 - y, core)

    def spread(begin, count, unroll, action, value):
        unroll = math.gcd(count, unroll)

        def several(j, carry):
            for u in range(unroll):
                carry = action(begin + j * unroll + u, carry)
            return carry

        return several(0, value) if unroll == count else lax.fori_loop(0, count // unroll, several, value)

    barrier = pltpu.get_barrier_semaphore()

    def greet(step, carry):
        pl.semaphore_signal(barrier, inc=1, device_id={"row": lax.rem(me + step, n)}, device_id_type=MESH)
        return carry

    lax.fori_loop(1, n, greet, 0)

    pieces = math.gcd(local, 4)
    per_piece = local // pieces

    def raw_load(i, p):
        slot = lax.rem(i, 2)
        return pltpu.make_async_copy(
            raw_ref.at[pl.ds(p * per_piece, per_piece), pl.ds(pl.multiple_of(i * block, block), block)],
            raw.at[slot, pl.ds(p * per_piece, per_piece)],
            raw_sem.at[slot, p],
        )

    def raw_start(i):
        for p in range(pieces):
            raw_load(i, p).start()

    def template_loads(g):
        bins = pl.ds(g * 2 * per_group, 2 * per_group)
        return [
            pltpu.make_async_copy(real_ref.at[bins], real.at[bins], load_sem.at[0, g]),
            pltpu.make_async_copy(imag_ref.at[bins], imag.at[bins], load_sem.at[1, g]),
        ]

    side_loads = [
        pltpu.make_async_copy(mask_ref, mask, side_sem.at[0]),
        pltpu.make_async_copy(move_ref, move, side_sem.at[1]),
    ]
    raw_start(0)
    if blocks > 1:
        raw_start(1)
    for copy in side_loads:
        copy.start()
    for g in range(groups):
        for copy in template_loads(g):
            copy.start()

    lane = lax.broadcasted_iota(jnp.int32, (8, 128), 1)
    low_half = lane < 2 * band
    total = jnp.zeros((samples, 128), jnp.float32)
    for i in range((taps + 1) // 2):
        odd = taps_ref[2 * i + 1] if 2 * i + 1 < taps else 0.0
        factor = jnp.where(low_half, taps_ref[2 * i], odd)[:1]
        total = total + factor * forward_ref[pl.ds(i, samples), :]
    high = total.astype(jnp.bfloat16).astype(jnp.float32)
    low = total - high
    half = low_half[:1]
    wide[pl.ds(0, samples, stride=2), :] = jnp.where(half, high, pltpu.roll(low, 2 * band, 1))
    wide[pl.ds(1, samples, stride=2), :] = jnp.where(half, pltpu.roll(high, 2 * band, 1), low)
    table[...] = wide[...].astype(jnp.bfloat16)
    if plan.rows * pairs != 2 * local * band:
        rows[...] = jnp.zeros_like(rows)

    def chunk(k, zo, yo):
        i, g = k // groups, lax.rem(k, groups)
        return gathered.at[i, core, zo * 2 + yo, pl.ds(g * per_group, per_group)]

    def shared_chunk(k, side):
        i, g = k // groups, lax.rem(k, groups)
        return gathered.at[i, side, :, pl.ds(g * per_group, per_group)]

    def send(k, zo, yo, target, slot):
        ref = chunk(k, zo, yo)
        return pltpu.make_async_remote_copy(
            src_ref=ref, dst_ref=ref, send_sem=send_sem.at[slot], recv_sem=recv_sem.at[k, zo * 2 + yo],
            device_id={"row": target}, device_id_type=MESH,
        )

    def give(k):
        ref = shared_chunk(k, core)
        return pltpu.make_async_remote_copy(
            src_ref=ref, dst_ref=ref, send_sem=give_sem.at[0], recv_sem=mate_sem.at[k],
            device_id={"row": partner}, device_id_type=MESH,
        )

    def arrived(k, zo, yo):
        send(k, zo, yo, partner, 0).wait_recv()

    near = layers == 4 and groups % 2 == 0
    sent = []

    def slot_of(condition=None, share=1):
        sent.append((condition, share))
        return len(sent) - 1

    def when(condition, action):
        if condition is None:
            action()
        else:
            pl.when(condition)(action)

    if near:
        far = z >= 2
        depth_of = jnp.where(far, 3 - z, z)
        inner, outer = depth_of == 1, depth_of == 0

        def at(q):
            return jnp.where(far, 3 - q, q)

        beside = 1 - depth_of
        own_slots = [(at(beside), None, slot_of()), (at(2), None, slot_of()), (at(3), inner, slot_of(inner))]
        own_across = slot_of()
        line_over = [slot_of(outer, 2), slot_of(), slot_of()]
        line_on = slot_of(inner)
        side_on_outer, side_on_inner = slot_of(outer), slot_of(inner, 2)

        def line_event(k, place, q):
            origin = at(q)
            arrived(k, origin, y)
            condition = outer & (lax.rem(k, 2) == 0) if place == 0 else None
            when(condition, lambda: send(k, origin, y, across, line_over[place]).start())
            if place == 2:
                when(inner, lambda: send(k, origin, y, index(at(0), y, core), line_on).start())

        def direct_events(k):
            line_event(k, 0, beside)
            line_event(k, 1, 2)
            pl.when(inner)(lambda: line_event(k, 2, 3))
            arrived(k, z, 1 - y)
            when(outer, lambda: send(k, z, 1 - y, index(at(1), y, core), side_on_outer).start())
            odd = inner & (lax.rem(k, 2) == 1)
            when(odd, lambda: send(k, z, 1 - y, index(at(0), y, core), side_on_inner).start())

        def second_events(k):
            pl.when(outer)(lambda: line_event(k, 2, 3))
            arrived(k, at(beside), 1 - y)
            arrived(k, at(2), 1 - y)

        def third_events(k):
            arrived(k, at(3), 1 - y)
            give(k).start()
    else:
        offsets = range(1, layers)
        own_slots = [(lax.rem(z + s, layers), None, slot_of()) for s in offsets]
        own_across = slot_of()
        line_over = [slot_of() for _ in offsets]

        def direct_events(k):
            for place, s in enumerate(offsets):
                origin = lax.rem(z + s, layers)
                arrived(k, origin, y)
                send(k, origin, y, across, line_over[place]).start()

        def second_events(k):
            for s in range(layers):
                origin = lax.rem(z + s, layers)
                arrived(k, origin, 1 - y)

        def third_events(k):
            give(k).start()

    def own_events(k):
        send(k, z, y, across, own_across).start()
        for target, condition, number in own_slots:
            when(condition, lambda: send(k, z, y, index(target, y, core), number).start())

    def front(i, carry):
        slot = lax.rem(i, 2)
        weights = table[...]
        for c in range(local):
            if c % per_piece == 0:
                raw_load(i, c // per_piece).wait()
            trace = raw[slot, c]
            upper = trace.astype(jnp.bfloat16)
            lower = (trace - upper.astype(jnp.float32)).astype(jnp.bfloat16)
            spectra = jnp.dot(
                jnp.concatenate([upper, lower], axis=0), weights, preferred_element_type=jnp.float32
            )
            turned = (spectra[:block] + spectra[block:]).T
            value = turned[: 2 * band] + turned[2 * band :]
            for part in range(2):
                place = plan.order.index((part, c))
                for parity in range(2):
                    at_row = part * band + parity * pairs
                    rows[pl.ds(plan.row_of(parity, place), pairs, stride=plan.row_pitch), :] = value[
                        at_row : at_row + pairs
                    ]

        @pl.when(i + 2 < blocks)
        def _():
            raw_start(i + 2)

        for g in range(pairs):
            gathered[i, core, me // 2, g] = rows[g * plan.row_pitch : g * plan.row_pitch + plan.rows, :].astype(jnp.bfloat16)

        @pl.when(i == 0)
        def _():
            pl.semaphore_wait(barrier, n - 1)

        for g in range(groups):
            k = i * groups + g
            pl.when(k < AHEAD)(lambda: own_events(k))
        return carry

    lax.fori_loop(0, blocks, front, 0)

    for copy in side_loads:
        copy.wait()
    turn = 2.0 * math.pi / samples
    shift = move[...]
    weight = mask[...].astype(jnp.float32)
    phase = turn * lax.rem(FIRST_BIN * shift, samples).astype(jnp.float32)
    cosine[...] = weight * jnp.cos(phase)
    sine[...] = weight * jnp.sin(phase)
    phase = turn * shift.astype(jnp.float32)
    cos_step[...] = jnp.cos(phase)
    sin_step[...] = jnp.sin(phase)
    square[...] = jnp.zeros_like(square)
    energy[...] = jnp.zeros_like(energy)
    lined[...] = jnp.zeros_like(lined)
    mine[...] = jnp.zeros_like(mine)

    sub = lax.broadcasted_iota(jnp.int32, (8, templates), 0)

    def eight(origin, start, swap):
        wanted = plan.order[start : start + 8]
        result = None
        at_row = 0
        while at_row < 8:
            if at_row >= len(wanted):
                piece = jnp.zeros((8, templates), jnp.float32)
                end = 8
            else:
                part, c = wanted[at_row]
                end = at_row
                while end < len(wanted) and wanted[end] == (part, c + end - at_row):
                    end += 1
                source = 1 - part if swap else part
                piece = lined[pl.ds(8 + source * channels + origin * local + c - at_row, 8), :]
                if swap and part == 0:
                    piece = -piece
            result = piece if result is None else jnp.where(sub < at_row, result, piece)
            at_row = end
        return result

    def prepare(f, parity):
        c, s = cosine[...], sine[...]
        a = real[f].astype(jnp.float32)
        b = imag[f].astype(jnp.float32)
        whole_real = (a * c + b * s).astype(jnp.bfloat16).astype(jnp.float32)
        whole_imag = (b * c - a * s).astype(jnp.bfloat16).astype(jnp.float32)
        power = whole_real * whole_real + whole_imag * whole_imag
        square[...] += jnp.sum(power.reshape(channels // 8, 8, templates), axis=0)
        lined[pl.ds(8, channels), :] = whole_real
        lined[pl.ds(8 + channels, channels), :] = whole_imag
        c1, s1 = cos_step[...], sin_step[...]
        cosine[...] = c * c1 - s * s1
        sine[...] = s * c1 + c * s1
        blank = jnp.zeros((8, templates), jnp.float32)
        for swap in range(2):
            for tile in range(plan.tiles):
                parts = []
                for origin in [chip * 2 + side for side in range(2) for chip in range(n // 2)]:
                    if tile < plan.full or not plan.shared:
                        pair = [eight(origin, tile * TILE, swap == 1), eight(origin, tile * TILE + 8, swap == 1)]
                    else:
                        pair = [blank, blank]
                        pair[parity] = eight(origin, tile * TILE, swap == 1)
                    parts += pair
                turned = jnp.concatenate(parts, axis=0).astype(jnp.bfloat16).T
                eff[f, swap * templates : (swap + 1) * templates, tile * n * TILE : (tile + 1) * n * TILE] = turned

    def prepare_group(g):
        for copy in template_loads(g):
            copy.wait()

        def one(p, carry):
            for parity in range(2):
                prepare(2 * p + parity, parity)
            return carry

        lax.fori_loop(g * per_group, (g + 1) * per_group, one, 0)

    def cross_chunk(k):
        i, g = k // groups, lax.rem(k, groups)
        slot = lax.rem(i, 2)
        mates = shared_chunk(k, 1 - core)
        pltpu.make_async_copy(mates, mates, mate_sem.at[k]).wait()

        def one(p, carry):
            tiles = {}

            def load(row):
                if row not in tiles:
                    tiles[row] = gathered[i, :, :, p, row : row + TILE, :].reshape(n * TILE, block)
                return tiles[row]

            for parity in range(2):
                f = 2 * p + parity
                spec = jnp.concatenate([load(plan.tile_row(parity, tile)) for tile in range(plan.tiles)], axis=0)
                both = jnp.dot(eff[f], spec, preferred_element_type=jnp.float32)
                cross[slot, pl.ds(f, templates, stride=plan.pitch), :] = both[:templates]
                cross[slot, pl.ds(band + f, templates, stride=plan.pitch), :] = both[templates:]
            power = jnp.zeros((8, block), jnp.float32)
            for tile in tiles.values():
                value = tile.astype(jnp.float32)
                power += jnp.sum((value * value).reshape(n * TILE // 8, 8, block), axis=0)
            energy[i] += power
            return carry

        spread(g * per_group, per_group, CROSS_UNROLL, one, 0)

    scale = math.sqrt(2.0 * channels * band)
    octets = templates // 8 // groups

    def peak_part(q):
        i, part = q // groups, lax.rem(q, groups)
        peak_range(i, part * octets, octets, PEAK_UNROLL, part == 0)

    def peak_range(i, begin, count, unroll, fresh):
        slot = lax.rem(i, 2)
        inverse = inverse_ref[...]
        data_norm = jnp.sqrt(jnp.sum(energy[i], axis=0, keepdims=True) + epsilon)

        def octet(j, carry):
            bank = lax.rem(j, 4)
            for t in range(0, 8, 2):
                joined = jnp.concatenate(
                    [
                        cross[slot, pl.ds(pl.multiple_of((j * 8 + t + u) * plan.pitch, 8), 2 * band), :]
                        for u in range(2)
                    ],
                    axis=1,
                )
                upper = joined.astype(jnp.bfloat16)
                lower = (joined - upper.astype(jnp.float32)).astype(jnp.bfloat16)
                stacked = jnp.dot(
                    inverse, jnp.concatenate([upper, lower, upper], axis=0), preferred_element_type=jnp.float32
                )
                top = jnp.max(stacked.reshape(samples // 8, 8, 2 * block), axis=0)
                tops[bank, 8 * t : 8 * t + 8, :] = top[:, :block]
                tops[bank, 8 * t + 8 : 8 * t + 16, :] = top[:, block:]
            here = pl.ds(pl.multiple_of(j * 8, 8), 8)
            value = tops[bank, pl.ds(0, 8, stride=8), :]
            for s in range(1, 8):
                value = jnp.maximum(value, tops[bank, pl.ds(s, 8, stride=8), :])
            value = value * scale / (norm[here, :] * data_norm)
            peak_ref[here, pl.ds(pl.multiple_of(i * block, block), block)] = value
            return jnp.maximum(carry, value)

        lowest = jnp.full((8, block), -jnp.inf, jnp.float32)
        largest = spread(begin, count, unroll, octet, lowest)
        largest = jnp.max(largest, axis=0, keepdims=True)
        row = pl.ds(i, 1)
        mine[row, :] = jnp.where(fresh, largest, jnp.maximum(mine[row, :], largest))

    peak_lag = CROSS + groups - 1

    def step(order, k, carry):
        def guarded(condition, action, index):
            pl.when(condition)(lambda: action(index))

        def finish_norm(k):
            total = jnp.sum(square[...], axis=0, keepdims=True)
            norm[...] = jnp.broadcast_to(jnp.sqrt(total + epsilon), (block, templates)).T

        def catch_up(k):
            for u in range(2):
                peak_part(2 * k - chunks - peak_lag + u)

        work = {
            "cross": (k >= CROSS, cross_chunk, k - CROSS),
            "peak": (k >= peak_lag, peak_part, k - peak_lag),
            "own": (k + AHEAD < chunks, own_events, k + AHEAD),
            "direct": (k < chunks, direct_events, k),
            "second": ((k >= LAG) & (k < chunks + LAG), second_events, k - LAG),
            "third": ((k >= 2 * LAG) & (k < chunks + 2 * LAG), third_events, k - 2 * LAG),
            "prepare": (k < groups, prepare_group, k),
            "catch_up": ((k < chunks + LAG) & (2 * k >= chunks + peak_lag), catch_up, k),
            "norm": (k == groups, finish_norm, k),
        }
        for name in order:
            guarded(*work[name])
        return carry

    lax.fori_loop(0, chunks, functools.partial(step, ORDER), 0)
    lax.fori_loop(chunks, chunks + CROSS, functools.partial(step, LATE), 0)

    peak_range(blocks - 1, 0, templates // 8, LAST_UNROLL, True)

    def best_copy(step):
        return pltpu.make_async_remote_copy(
            src_ref=mine, dst_ref=slots.at[step - 1], send_sem=best_send.at[0], recv_sem=best_recv.at[0],
            device_id={"row": lax.rem(me + step, n)}, device_id_type=MESH,
        )

    def best_start(step, carry):
        best_copy(step).start()
        return carry

    lax.fori_loop(1, n, best_start, 0)
    for number, (condition, share) in enumerate(sent):
        ref = gathered.at[:, 0, 0] if share == 1 else gathered.at[:, 0, 0, pl.ds(0, pairs // share)]
        wait = pltpu.make_async_remote_copy(
            src_ref=ref, dst_ref=ref, send_sem=send_sem.at[number], recv_sem=recv_sem.at[0, 0],
            device_id={"row": partner}, device_id_type=MESH,
        )
        when(condition, wait.wait_send)
    whole = gathered.at[:, 0]
    pltpu.make_async_remote_copy(
        src_ref=whole, dst_ref=whole, send_sem=give_sem.at[0], recv_sem=recv_sem.at[0, 0],
        device_id={"row": partner}, device_id_type=MESH,
    ).wait_send()
    everyone = slots.at[pl.ds(0, n - 1)]
    all_best = pltpu.make_async_remote_copy(
        src_ref=everyone, dst_ref=everyone, send_sem=best_send.at[0], recv_sem=best_recv.at[0],
        device_id={"row": partner}, device_id_type=MESH,
    )
    all_best.wait()
    best_ref[...] = jnp.maximum(mine[...], jnp.max(slots[...], axis=0))


def finish_kernel(blocks, peak_ref, best_ref, peak_out, best_out):
    block = best_ref.shape[1]
    for i in range(blocks):
        best_out[pl.ds(i * block, block)] = best_ref[i]
    peak_out[...] = peak_ref[...]


def send_slots(plan):
    if plan.layers == 4 and plan.groups % 2 == 0:
        return 10
    return 2 * plan.layers - 1


def body(n, raw_trace, fir_taps, templ_real, templ_imag, channel_mask, moveout):
    local, windows, length = raw_trace.shape
    samples = length // 2
    band, channels, templates = templ_real.shape
    plan = Plan(n, local, band, samples, templates, windows)
    bins = FIRST_BIN + np.arange(band)
    lags = np.arange(samples)
    angle = 2.0 * np.pi / samples * (bins[:, None] * lags[None, :] % samples)
    inverse = np.concatenate([np.cos(angle), -np.sin(angle)], axis=0)

    span = (fir_taps.shape[0] + 1) // 2
    forward = np.zeros((samples + span + 1, 2 * band))
    forward[:samples] = np.concatenate([inverse[:band][::2], inverse[:band][1::2], inverse[band:][::2], inverse[band:][1::2]]).T
    padded = -(-(samples + span) // 8) * 8
    both = np.zeros((padded, 4 * band), np.float32)
    both[: samples + span, : 2 * band] = forward[:-1]
    both[: samples + span, 2 * band :] = forward[1:]
    forward = jnp.asarray(both)

    inverse = inverse.T.astype(np.float32)
    high = inverse.astype(jnp.bfloat16)
    low = (inverse - high.astype(np.float32)).astype(jnp.bfloat16)
    inverse3 = jnp.asarray(np.concatenate([high, high, low], axis=1))

    vmem = pl.BlockSpec(memory_space=pltpu.VMEM)
    anywhere = pl.BlockSpec(memory_space=pl.ANY)
    f32, bf16 = jnp.float32, jnp.bfloat16
    pieces = math.gcd(local, 4)
    best_rows = -(-plan.blocks // 8) * 8
    peak, best = pl.pallas_call(
        functools.partial(scan_kernel, plan),
        out_shape=(
            jax.ShapeDtypeStruct((templates, windows), f32),
            jax.ShapeDtypeStruct((best_rows, plan.block), f32),
        ),
        in_specs=[pl.BlockSpec(memory_space=pltpu.SMEM), vmem, vmem] + [anywhere] * 5,
        out_specs=(vmem, vmem),
        scratch_shapes=[
            pltpu.VMEM((plan.blocks, 2, n // 2, plan.pairs, plan.rows, plan.block), bf16),
            pltpu.VMEM((band, 2 * templates, plan.depth), bf16),
            pltpu.VMEM((2, templates * plan.pitch, plan.block), f32),
            pltpu.VMEM((2, local, plan.block, length), f32),
            pltpu.VMEM((length, 4 * band), bf16),
            pltpu.VMEM((length, 4 * band), f32),
            pltpu.VMEM((plan.pairs * plan.row_pitch, plan.block), f32),
            pltpu.VMEM((band, channels, templates), bf16),
            pltpu.VMEM((band, channels, templates), bf16),
            pltpu.VMEM((channels, templates), jnp.int32),
            pltpu.VMEM((channels, templates), jnp.int32),
            pltpu.VMEM((channels, templates), f32),
            pltpu.VMEM((channels, templates), f32),
            pltpu.VMEM((channels, templates), f32),
            pltpu.VMEM((channels, templates), f32),
            pltpu.VMEM((2 * channels + 16, templates), f32),
            pltpu.VMEM((8, templates), f32),
            pltpu.VMEM((plan.blocks, 8, plan.block), f32),
            pltpu.VMEM((templates, plan.block), f32),
            pltpu.VMEM((4, 64, plan.block), f32),
            pltpu.VMEM((best_rows, plan.block), f32),
            pltpu.VMEM((n - 1, best_rows, plan.block), f32),
            pltpu.SemaphoreType.DMA((2, pieces)),
            pltpu.SemaphoreType.DMA((2,)),
            pltpu.SemaphoreType.DMA((2, plan.groups)),
            pltpu.SemaphoreType.DMA((plan.chunks, n // 2)),
            pltpu.SemaphoreType.DMA((plan.chunks,)),
            pltpu.SemaphoreType.DMA((1,)),
            pltpu.SemaphoreType.DMA((send_slots(plan),)),
            pltpu.SemaphoreType.DMA((1,)),
            pltpu.SemaphoreType.DMA((1,)),
        ],
        compiler_params=pltpu.CompilerParams(
            collective_id=0, has_side_effects=True, vmem_limit_bytes=VMEM_LIMIT
        ),
        name="gather_scan",
    )(fir_taps, forward, inverse3, channel_mask, moveout, raw_trace, templ_real, templ_imag)
    peak, best = pl.pallas_call(
        functools.partial(finish_kernel, plan.blocks),
        out_shape=(jax.ShapeDtypeStruct((templates, windows), f32), jax.ShapeDtypeStruct((windows,), f32)),
        in_specs=[vmem, vmem],
        out_specs=(vmem, vmem),

        name="finish",
    )(peak, best)
    return (peak, best)


def solution(mesh):
    in_specs = (
        P("row", "parts", None),
        P(),
        P(None, None, "row"),
        P(None, None, "row"),
        P(None, "row"),
        P(None, "row"),
    )
    out_specs = (P("row", "parts"), P("parts"))
    return jax.shard_map(
        functools.partial(body, mesh.shape["row"]),
        mesh=mesh,
        in_specs=in_specs,
        out_specs=out_specs,
        check_vma=False,
    )
```
